32 devices in a mesh: grp: 2 (over x), space: 16 (over z, y, core).
Axes of the slice: x: 2, y: 2, z: 4, core: 2. Of those that a mesh axis runs over, the one named last changes fastest.
Arguments:
- right_side: float32 [165, 12288], P(None, ('grp', 'space')), parts along dimension 1, may hold values from -48 to 48
- capacity: float32 [12288], P(('grp', 'space')), parts along dimension 0, may hold values from 0.5 to 2
- base_cond: float32 [192, 24, 4096], P(('grp', 'space')), parts along dimension 0, may hold values from 0.0005 to 0.005
- var_field: float32 [8, 12288], P(None, ('grp', 'space')), parts along dimension 1, may hold values from -1 to 1
- block_cols: int32 [192, 23], P(('grp', 'space')), parts along dimension 0, may hold values from 0 to 11, as said below
- send_list: int32 [32, 2, 3], P(('grp', 'space')), parts along dimension 0, may hold values from 0 to 5, as said below
Outputs:
- solution_field: float32 [165, 12288], P(None, ('grp', 'space')), parts along dimension 1
- residual: float32 [165, 12288], P(None, ('grp', 'space')), parts along dimension 1
The draws below stay inside these ranges and needn't reach their ends.
There are 2 independent parts, one for each index of `grp`. The reference program is written for one: setup_inputs(seed, part) draws one part's arguments, and reference() takes and returns one part's arrays. A program takes and returns all parts, laid end to end along the dimension named above; each array names one. Nothing has to cross between parts.
Inputs may be any that keep to these rules, and one draw needn't show every extreme that they name: `block_cols`: A value below 6 names a block of the same device; 6 + h names the h-th block that the previous device of space sends up, 9 + h the h-th block that the next device sends down. The first device never names the previous one, the last never names the next one; every other value occurs on every device. `send_list`: on every device the 6 blocks differ; block 5 is always sent up and block 0 always sent down.
All inputs are finite; a program needn't handle non-finite values.
Results may differ from the reference program's by a relative error of at most 0.0003.
Values sent between devices are 32-bit elements; how exact they have to be, the bound alone decides.
No kernel may reach another device: no remote copies, remote signals or barrier semaphores. Data moves between devices by JAX's collectives and lax.ppermute only.
A program may use at most 128 MiB of HBM per device.

```python
import math
import jax
import jax.numpy as jnp
import numpy as np
from jax import lax

VARS = 8
ORDER = 3
TERMS = 165
MODES = 9
BLK = 64
SLOTS = 24
HALO = 3
NB_DEV = 6
ITERS = 2
NBLOCKS = 96
NODES = 6144
N_SPACE = 16


def draw_right_side(key, part):
    key_core = jax.random.fold_in(key, 11)
    key_node = jax.random.fold_in(key, 12)
    key_term = jax.random.fold_in(key, 13)
    along = jnp.arange(NODES, dtype=jnp.float32) / (NODES - 1)
    node_scale = 10.0 ** (jax.random.uniform(key_node, (NODES,), jnp.float32) - 0.5)
    term_scale = 10.0 ** (jax.random.uniform(key_term, (TERMS, 1), jnp.float32) - 0.5)
    core = jnp.clip(jax.random.normal(key_core, (TERMS, NODES), jnp.float32), -3.0, 3.0)
    rising = 3.0 ** (along - 0.5)
    return (core * node_scale * rising * term_scale * 0.5).astype(jnp.float32)


def draw_block_cols(key, part):
    extent_ids = NB_DEV + 2 * HALO
    positions = NB_DEV * (SLOTS - 1)
    repeats = -(-positions // extent_ids)

    def one_device(device_key, device):
        pieces = [jax.random.permutation(jax.random.fold_in(device_key, t), extent_ids) for t in range(repeats)]
        sequence = jnp.concatenate(pieces)[:positions].astype(jnp.int32)
        lower_bad = (sequence >= NB_DEV) & (sequence < NB_DEV + HALO) & (device == 0)
        upper_bad = (sequence >= NB_DEV + HALO) & (device == N_SPACE - 1)
        sequence = jnp.where(lower_bad | upper_bad, sequence % NB_DEV, sequence)
        sequence = jax.random.permutation(jax.random.fold_in(device_key, 1000), sequence)
        return sequence.reshape(NB_DEV, SLOTS - 1)
    devices = jnp.arange(N_SPACE, dtype=jnp.int32)
    device_keys = jax.vmap(lambda d: jax.random.fold_in(key, d))(devices)
    return jax.vmap(one_device)(device_keys, devices).reshape(N_SPACE * NB_DEV, SLOTS - 1).astype(jnp.int32)


def draw_send_list(key, part):

    def one_device(device_key):
        ranks = jax.random.permutation(device_key, NB_DEV).astype(jnp.int32)
        places = jnp.arange(NB_DEV, dtype=jnp.int32)
        ranks = jnp.where(places == 0, -2, jnp.where(places == NB_DEV - 1, -1, ranks))
        order = jnp.argsort(ranks, stable=True).astype(jnp.int32)
        upward = order[1:HALO + 1]
        downward = jnp.concatenate([order[0:1], order[HALO + 1:2 * HALO]])
        return jnp.stack([upward, downward], axis=0)
    device_keys = jax.vmap(lambda d: jax.random.fold_in(jax.random.fold_in(key, 77), d))(jnp.arange(N_SPACE))
    return jax.vmap(one_device)(device_keys).astype(jnp.int32)


def block_scale(stream_key, dims, cuts, least, high):
    factor_of = 1.0
    for position, blocks in cuts:
        draws = jax.random.uniform(jax.random.fold_in(jax.random.fold_in(stream_key, 6), position), (blocks,), jnp.float32, least / len(cuts), high / len(cuts))
        factor_of = factor_of * jnp.repeat(jnp.exp(draws), dims[position] // blocks).reshape((-1,) + (1,) * (len(dims) - 1 - position))
    return factor_of


def setup_inputs(seed: int = 0, part: int = 0) -> dict:
    keys = jax.random.split(jax.random.key(seed), 7)
    part_keys = jax.random.split(jax.random.fold_in(keys[6], part), 7)
    return {
        "right_side": draw_right_side(jax.random.fold_in(jax.random.fold_in(keys[6], part), 71), part),
        "capacity": jnp.clip(jnp.exp(math.log(2.0) - 1.3862944 * jax.random.uniform(part_keys[1], (NODES,), jnp.float32) ** block_scale(part_keys[1], (NODES,), ((0, 16),), -0.2, 0.2)), 0.5, 2.0),
        "base_cond": jnp.clip(jnp.exp(math.log(0.005) - 2.30258502 * jax.random.uniform(part_keys[2], (NBLOCKS, SLOTS, BLK * BLK), jnp.float32) ** block_scale(part_keys[2], (NBLOCKS, SLOTS, BLK * BLK), ((0, 16),), -0.2, 0.2)), 0.0005, 0.005),
        "var_field": jnp.clip(jax.random.uniform(part_keys[3], (VARS, NODES), jnp.float32, -1.0, 1.0) * block_scale(part_keys[3], (VARS, NODES), ((1, 16),), -0.4, 0.0), -1.0, 1.0),
        "block_cols": draw_block_cols(jax.random.fold_in(jax.random.fold_in(keys[6], part), 71), part),
        "send_list": draw_send_list(jax.random.fold_in(jax.random.fold_in(keys[6], part), 71), part),
    }


spread_coefficient = 0.14

def chaos_tables():
    entries = []

    def grow(prefix, budget_left):
        if len(prefix) == VARS:
            entries.append(tuple(prefix))
            return
        for degree in range(budget_left + 1):
            grow(prefix + [degree], budget_left - degree)
    grow([], ORDER)
    entries.sort(key=lambda multi_index: (sum(multi_index), tuple((-v for v in multi_index))))
    lookup = {multi_index: place for place, multi_index in enumerate(entries)}
    count_terms = len(entries)
    down_index = np.full((VARS, count_terms), count_terms, np.int32)
    down_scale = np.zeros((VARS, count_terms), np.float32)
    up_index = np.full((VARS, count_terms), count_terms, np.int32)
    up_scale = np.zeros((VARS, count_terms), np.float32)
    for place, multi_index in enumerate(entries):
        for k in range(VARS):
            if multi_index[k] > 0:
                lowered = multi_index[:k] + (multi_index[k] - 1,) + multi_index[k + 1:]
                down_index[k, place] = lookup[lowered]
                down_scale[k, place] = math.sqrt(multi_index[k])
            raised = multi_index[:k] + (multi_index[k] + 1,) + multi_index[k + 1:]
            if raised in lookup:
                up_index[k, place] = lookup[raised]
                up_scale[k, place] = math.sqrt(multi_index[k] + 1)
    return (down_index, down_scale, up_index, up_scale)

def couple(field, mode_weights):
    down_index, down_scale, up_index, up_scale = chaos_tables()
    padded = jnp.concatenate([field, jnp.zeros((1,) + field.shape[1:], field.dtype)], axis=0)
    total = mode_weights[0] * field
    for k in range(VARS):
        lowered = jnp.take(padded, down_index[k], axis=0) * down_scale[k][:, None, None]
        raised = jnp.take(padded, up_index[k], axis=0) * up_scale[k][:, None, None]
        total = total + mode_weights[k + 1] * (lowered + raised)
    return total

def reference(right_side, capacity, base_cond, var_field, block_cols, send_list):
    blocks = NB_DEV * N_SPACE
    base_cond = base_cond.reshape(blocks, SLOTS, BLK, BLK)
    owner = jnp.arange(blocks, dtype=jnp.int32) // NB_DEV
    own_index = jnp.arange(blocks, dtype=jnp.int32) % NB_DEV
    local_ids = jnp.concatenate([own_index[:, None], block_cols], axis=1)
    lower_slot = jnp.clip(local_ids - NB_DEV, 0, HALO - 1)
    upper_slot = jnp.clip(local_ids - NB_DEV - HALO, 0, HALO - 1)
    lower_peer = jnp.clip(owner - 1, 0, N_SPACE - 1)[:, None]
    upper_peer = jnp.clip(owner + 1, 0, N_SPACE - 1)[:, None]
    from_lower = lower_peer * NB_DEV + send_list[lower_peer, 0, lower_slot]
    from_upper = upper_peer * NB_DEV + send_list[upper_peer, 1, upper_slot]
    columns = jnp.where(local_ids < NB_DEV, owner[:, None] * NB_DEV + local_ids, jnp.where(local_ids < NB_DEV + HALO, from_lower, from_upper)).astype(jnp.int32)
    mode_weights = jnp.concatenate([jnp.ones((1, NODES), jnp.float32), spread_coefficient * var_field], axis=0)
    mode_weights = mode_weights.reshape(MODES, blocks, BLK)
    row_total = lax.optimization_barrier(jnp.sum(base_cond, axis=(1, 3)))
    column_total = jnp.einsum('rsab,mra->mrsb', base_cond, mode_weights, precision=lax.Precision.HIGHEST)
    transfer = jnp.zeros((MODES, blocks, BLK), jnp.float32).at[:, columns.reshape(-1)].add(column_total.reshape(MODES, blocks * SLOTS, BLK))
    cap_blocks = capacity.reshape(blocks, BLK)

    def operate(field):

        def group_step(accum, g):
            start = g * NB_DEV
            piece = lax.dynamic_slice_in_dim(field, start, NB_DEV, 1)
            group_cols = lax.dynamic_slice_in_dim(columns, start, NB_DEV, 0)
            group_base = lax.dynamic_slice_in_dim(base_cond, start, NB_DEV, 0)
            group_weights = lax.dynamic_slice_in_dim(mode_weights, start, NB_DEV, 1)
            group_rows = lax.dynamic_slice_in_dim(row_total, start, NB_DEV, 0)
            neighbours = jnp.take(field, group_cols, axis=1)
            outflow = group_rows * piece - jnp.einsum('rsab,prsb->pra', group_base, neighbours, precision=lax.Precision.HIGHEST)
            forward = couple(outflow, group_weights)
            coupled = couple(piece, group_weights)
            inflow = jnp.einsum('rsab,pra->prsb', group_base, coupled, precision=lax.Precision.HIGHEST)
            accum = accum.at[:, group_cols.reshape(-1)].add(-inflow.reshape(TERMS, NB_DEV * SLOTS, BLK))
            current = lax.dynamic_slice_in_dim(accum, start, NB_DEV, 1)
            accum = lax.dynamic_update_slice_in_dim(accum, current + forward, start, 1)
            return (accum, None)
        initial = cap_blocks * field + couple(field, transfer)
        result, unused = lax.scan(group_step, initial, jnp.arange(N_SPACE, dtype=jnp.int32))
        return result
    source_field = right_side.reshape(TERMS, blocks, BLK)
    solution_field = jnp.zeros_like(source_field)
    residual = source_field
    direction = source_field
    norm_now = jnp.sum(residual * residual)
    for step in range(ITERS):
        image = operate(direction)
        step_length = norm_now / jnp.sum(direction * image)
        solution_field = solution_field + step_length * direction
        residual = residual - step_length * image
        norm_next = jnp.sum(residual * residual)
        direction = residual + norm_next / norm_now * direction
        norm_now = norm_next
    return (solution_field.reshape(TERMS, NODES), residual.reshape(TERMS, NODES))
```

```python
import functools
import math

import jax
import jax.numpy as jnp
from jax import lax
from jax.experimental import pallas as pl
from jax.experimental.pallas import tpu as pltpu
from jax.sharding import PartitionSpec as P

VARS = 8
ORDER = 3
LANES = 128
SPREAD = 0.14
F32 = jnp.float32
BF16 = jnp.bfloat16


@functools.cache
def chaos_links():
    entries = []

    def grow(prefix, budget_left):
        if len(prefix) == VARS:
            entries.append(tuple(prefix))
            return
        for degree in range(budget_left + 1):
            grow(prefix + [degree], budget_left - degree)

    grow([], ORDER)
    entries.sort(key=lambda beta: (sum(beta), tuple(-v for v in beta)))
    lookup = {beta: place for place, beta in enumerate(entries)}
    links = []
    for beta in entries:
        mine = []
        for k in range(VARS):
            if beta[k] > 0:
                lowered = beta[:k] + (beta[k] - 1,) + beta[k + 1 :]
                mine.append((k, lookup[lowered], beta[k]))
            raised = beta[:k] + (beta[k] + 1,) + beta[k + 1 :]
            if raised in lookup:
                mine.append((k, lookup[raised], beta[k] + 1))
        links.append(mine)
    return links


def split(value):
    high = value.astype(BF16)
    return high, (value - high.astype(F32)).astype(BF16)


def product(high, low, w_high, w_low, dims):
    rows = high.shape[0]
    both = jnp.concatenate([high, low], axis=0)
    dot = functools.partial(lax.dot_general, dimension_numbers=(dims, ((), ())), preferred_element_type=F32)
    main = dot(both, w_high)
    return main[:rows] + (main[rows:] + dot(high, w_low))


def couple(source, target, coefs):
    first = coefs[0]
    scaled = {}
    for k in range(VARS):
        for square in range(1, ORDER + 1):
            scaled[k, square] = coefs[k + 1] if square == 1 else coefs[k + 1] * math.sqrt(square)
    for term, mine in enumerate(chaos_links()):
        total = source[term * 8 : term * 8 + 8, :]
        if first is not None:
            total = total * first
        for k, other, square in mine:
            total = total + scaled[k, square] * source[other * 8 : other * 8 + 8, :]
        target[term * 8 : term * 8 + 8, :] = total


def spread_rows(target, chunk, value):
    target[pl.ds(chunk, value.shape[0], stride=8), :] = value


def lane_iota(shape):
    return lax.broadcasted_iota(jnp.int32, shape, len(shape) - 1)


def row_iota(shape):
    return lax.broadcasted_iota(jnp.int32, shape, 0)


def pick_block(ref, place, half, rows):
    tile = ref[0:rows, pl.ds(pl.multiple_of((place // 2) * LANES, LANES), LANES)]
    return jnp.where(place % 2 == half, tile, pltpu.roll(tile, LANES // 2, 1))


def permute_blocks(ref, places, chunk, rows):
    left = pick_block(ref, places[2 * chunk], 0, rows)
    right = pick_block(ref, places[2 * chunk + 1], 1, rows)
    return jnp.where(lane_iota(left.shape) < LANES // 2, left, right)


def build_kernel(
    cols, sends, field, cap, var, base,
    w_high, w_low, field_p, pay_up, pay_down, own_part, aux,
    buf, turned, acc, dense, major, coupled_major, coef_major, place, sems,
):
    blocks, slots, flat = base.shape
    terms, nodes = field.shape
    tall = field_p.shape[0]
    width = nodes // blocks
    steps = flat // LANES
    chunks = nodes // LANES
    order = [sends[0, j // (blocks // 2), j % (blocks // 2)] for j in range(blocks)]
    copies = [pltpu.make_async_copy(base.at[order[j]], buf.at[j], sems.at[j]) for j in range(blocks)]
    for copy in copies:
        copy.start()

    for j in range(2 * blocks):
        place[j] = j
    for j in range(blocks):
        place[order[j]] = j

    aux[...] = jnp.zeros_like(aux)
    for chunk in range(chunks):
        lanes = slice(chunk * LANES, (chunk + 1) * LANES)
        piece = permute_blocks(field, order, chunk, terms)
        field_p[0:terms, lanes] = piece
        field_p[terms:tall, lanes] = jnp.zeros((tall - terms, LANES), F32)
        spread_rows(major, chunk, field_p[:, lanes])
        weights = permute_blocks(var, order, chunk, VARS) * SPREAD
        aux[0:VARS, lanes] = weights
        aux[VARS : VARS + 1, lanes] = permute_blocks(cap, order, chunk, 1)
        spread_rows(coef_major, chunk, weights)
    coefs = [None] + [coef_major[k * 8 : k * 8 + 8, :] for k in range(VARS)]
    couple(major, coupled_major, coefs)

    for one in acc:
        one[...] = jnp.zeros_like(one)
    for j in range(blocks):
        copies[j].wait()
        for step in range(steps):
            turned[j, pl.ds(step, slots, stride=steps), :] = buf[j, :, step * LANES : (step + 1) * LANES]
    for slot in range(slots):
        for j in range(blocks):
            where = j if slot == 0 else place[cols[order[j], slot - 1]]
            acc[j][where] += turned[j, slot * steps : (slot + 1) * steps, :]
    for j in range(blocks):
        for pair in range(blocks):
            even, odd = acc[j][2 * pair], acc[j][2 * pair + 1]
            near = lane_iota(even.shape) < width
            start = pair * nodes + j * width
            dense[pl.ds(start, steps, stride=2), :] = jnp.where(near, even, pltpu.roll(odd, width, 1))
            dense[pl.ds(start + 1, steps, stride=2), :] = jnp.where(near, pltpu.roll(even, width, 1), odd)
    for pair in range(blocks):
        lanes = slice(pair * LANES, (pair + 1) * LANES)
        w_high[:, lanes], w_low[:, lanes] = split(dense[pair * nodes : (pair + 1) * nodes, :])
    high, low = w_high[...], w_low[...]

    rows = []
    for chunk in range(chunks):
        piece = coupled_major[pl.ds(chunk, tall, stride=8), :]
        where = row_iota(piece.shape)
        rows.append(jnp.where(where < terms, piece, jnp.where(where == terms, 1.0, 0.0)))
    left = jnp.concatenate([jnp.concatenate(rows, axis=1), aux[0:VARS, :]], axis=0)
    left_high, left_low = split(left)
    flux = product(left_high, left_low, high, low, ((1,), (0,)))
    own_part[...] = flux[:, 0:nodes]
    outer = flux[:, nodes:]
    near = lane_iota((outer.shape[0], nodes)) < nodes // 2
    grown = jnp.concatenate([field_p[...], jnp.zeros((outer.shape[0] - tall, nodes), F32)], axis=0)
    where = row_iota(outer.shape)
    grown = jnp.where(where < terms, grown, 0.0)
    transfer = where >= terms
    pay_up[...] = jnp.where(near, grown, outer)
    pay_down[...] = jnp.where(near, outer, grown)


def apply_kernel(
    first, peers,
    w_high, w_low, field, own_part, aux, coef_in, from_below, from_above, *refs,
):
    if first:
        image, flux_own, pay_up, pay_down, coef_out, dots, major, result, single = refs
    else:
        field0, dots_in, image, dots, major, result = refs
    tall, nodes = field.shape
    terms = len(chaos_links())
    chunks = nodes // LANES
    below, above = from_below[0:tall, :], from_above[0:tall, :]
    near = lane_iota(below.shape) < nodes // 2
    where = row_iota(below.shape)
    halo = jnp.where(near, below, above)
    inward = jnp.where(near, above, below)
    value = field[...]
    extended = jnp.concatenate([value, halo], axis=1)
    marked = jnp.where(row_iota(extended.shape) < terms, extended, jnp.where(row_iota(extended.shape) == terms, 1.0, 0.0))
    ext_high, ext_low = split(marked)
    mixed = product(ext_high, ext_low, w_high[...], w_low[...], ((1,), (1,)))
    outflow = mixed[terms : terms + 1, :] * value - mixed

    if first:
        ones = jnp.ones((1, LANES), F32)
        wide = lane_iota((1, nodes)) < nodes // 2
        total0 = own_part[terms : terms + 1, :] + jnp.where(
            wide, from_above[terms : terms + 1, :], from_below[terms : terms + 1, :]
        )
        wide = lane_iota((VARS, nodes)) < nodes // 2
        totals = own_part[tall : tall + VARS, :] + jnp.where(
            wide, from_above[tall : tall + VARS, :], from_below[tall : tall + VARS, :]
        )
        coef = coef_out
        coef[...] = jnp.zeros_like(coef)
        for chunk in range(chunks):
            lanes = slice(chunk * LANES, (chunk + 1) * LANES)
            coef[chunk : chunk + 1, :] = ones
            coef[chunks + chunk : chunks + chunk + 1, :] = total0[:, lanes]
            coef[pl.ds(8 + chunk, VARS, stride=8), :] = aux[0:VARS, lanes]
            coef[pl.ds(8 + chunks + chunk, VARS, stride=8), :] = totals[:, lanes]
    else:
        coef = coef_in
    for chunk in range(chunks):
        lanes = slice(chunk * LANES, (chunk + 1) * LANES)
        spread_rows(major, chunk, outflow[:, lanes])
        spread_rows(major, chunks + chunk, value[:, lanes])
    couple(major, result, [coef[k * 8 : k * 8 + 8, :] for k in range(VARS + 1)])
    pieces = []
    for chunk in range(chunks):
        pieces.append(
            result[pl.ds(chunk, tall, stride=8), :] + result[pl.ds(chunks + chunk, tall, stride=8), :]
        )
    out = aux[VARS : VARS + 1, :] * value + jnp.concatenate(pieces, axis=1) - (own_part[0:tall, :] + inward)
    out = jnp.where(where < terms, out, 0.0)
    image[...] = out

    def dot(a, b):
        lanes_sum = jnp.sum(a * b, axis=0, keepdims=True)
        total = lanes_sum[:, 0:LANES]
        for chunk in range(1, chunks):
            total = total + lanes_sum[:, chunk * LANES : (chunk + 1) * LANES]
        return total

    if first:
        dots[...] = jnp.zeros_like(dots)
        dots[0:1, :] = dot(value, value)
        dots[1:2, :] = dot(value, out)
        dots[2:3, :] = dot(out, out)
        for chunk in range(chunks):
            spread_rows(single, chunk, out[:, chunk * LANES : (chunk + 1) * LANES])
        couple(single, result, [None] + [coef[k * 8 + 8 : k * 8 + 16, :] for k in range(VARS)])
        rows = []
        for chunk in range(chunks):
            piece = result[pl.ds(chunk, tall, stride=8), :]
            rows.append(jnp.where(row_iota(piece.shape) < terms, piece, 0.0))
        c_high, c_low = split(jnp.concatenate(rows, axis=1))
        flux = product(c_high, c_low, w_high[...], w_low[...], ((1,), (0,)))
        flux_own[...] = flux[:, 0:nodes]
        outer = flux[:, nodes:]
        pay_up[...] = jnp.where(near, out, outer)
        pay_down[...] = jnp.where(near, outer, out)
    else:
        all_dots = dots_in[...]
        row = row_iota(all_dots.shape)
        all_dots = jnp.where(row == 3, dot(field0[...], out), all_dots)
        all_dots = jnp.where(row == 4, dot(value, out), all_dots)
        for peer in range(peers):
            dots[peer * 8 : peer * 8 + 8, :] = all_dots


def final_kernel(peers, sends, dots, field, image, image2, solution_out, residual_out, place, work):
    terms, nodes = solution_out.shape
    halves = sends.shape[2]
    blocks = 2 * halves
    chunks = nodes // LANES
    for j in range(blocks):
        place[sends[0, j // halves, j % halves]] = j
    places = [place[j] for j in range(blocks)]
    total = dots[0:8, :]
    for peer in range(1, peers):
        total = total + dots[peer * 8 : peer * 8 + 8, :]

    def add(row):
        return jnp.sum(row, axis=1, keepdims=True)

    bb, by, yy, bz, yz = (total[k : k + 1, :] for k in range(5))
    norm = add(bb)
    step0 = norm / add(by)
    norm1 = add(bb - step0 * (2.0 * by - step0 * yy))
    ratio = norm1 / norm
    grow = 1.0 + ratio
    curve = add(grow * grow * by - step0 * (grow * (bz + yy) - step0 * yz))
    step1 = norm1 / curve
    c1 = step0 + step1 * grow
    c2 = step0 * step1
    work[0] = c1 * field[...] - c2 * image[...]
    work[1] = field[...] - c1 * image[...] + c2 * image2[...]
    for which, out in enumerate((solution_out, residual_out)):
        for chunk in range(chunks):
            out[:, chunk * LANES : (chunk + 1) * LANES] = permute_blocks(work.at[which], places, chunk, terms)


def vmem(count):
    return [pl.BlockSpec(memory_space=pltpu.VMEM)] * count


def smem(count):
    return [pl.BlockSpec(memory_space=pltpu.SMEM)] * count


def shape(dims, dtype=F32):
    return jax.ShapeDtypeStruct(dims, dtype)


def shift(value, steps):
    count = lax.axis_size("space")
    pairs = [(i, i + steps) for i in range(max(0, -steps), min(count, count - steps))]
    return lax.ppermute(value, "space", pairs)


def shards(right_side, capacity, base_cond, var_field, block_cols, send_list):
    blocks, slots, flat = base_cond.shape
    terms, nodes = right_side.shape
    peers = lax.axis_size("space")
    tall = -(-terms // 8) * 8
    steps = flat // LANES
    params = pltpu.CompilerParams(vmem_limit_bytes=48 * 1024 * 1024)

    w_high, w_low, field, pay_up, pay_down, own_part, aux = pl.pallas_call(
        build_kernel,
        out_shape=(
            shape((nodes, 2 * nodes), BF16),
            shape((nodes, 2 * nodes), BF16),
            shape((tall, nodes)),
            shape((tall + VARS, nodes)),
            shape((tall + VARS, nodes)),
            shape((tall + VARS, nodes)),
            shape((2 * VARS, nodes)),
        ),
        in_specs=smem(2) + vmem(3) + [pl.BlockSpec(memory_space=pl.ANY)],
        out_specs=tuple(vmem(7)),
        scratch_shapes=[
            pltpu.VMEM((blocks, slots, flat), F32),
            pltpu.VMEM((blocks, slots * steps, LANES), F32),
            [pltpu.VMEM((2 * blocks, steps, LANES), F32) for _ in range(blocks)],
            pltpu.VMEM((blocks * nodes, LANES), F32),
            pltpu.VMEM((tall * 8, LANES), F32),
            pltpu.VMEM((tall * 8, LANES), F32),
            pltpu.VMEM((VARS * 8, LANES), F32),
            pltpu.SMEM((2 * blocks,), jnp.int32),
            pltpu.SemaphoreType.DMA((blocks,)),
        ],
        compiler_params=params,
        name="build",
    )(block_cols, send_list, right_side, capacity.reshape(1, nodes), var_field, base_cond)

    from_below = shift(pay_up, 1)
    from_above = shift(pay_down, -1)
    image, flux_own, pay_up, pay_down, coef, dots = pl.pallas_call(
        functools.partial(apply_kernel, True, peers),
        out_shape=(
            shape((tall, nodes)),
            shape((tall, nodes)),
            shape((tall, nodes)),
            shape((tall, nodes)),
            shape((8 * (VARS + 1), LANES)),
            shape((8, LANES)),
        ),
        in_specs=vmem(8),
        out_specs=tuple(vmem(6)),
        scratch_shapes=[pltpu.VMEM((tall * 8, LANES), F32)] * 3,
        compiler_params=params,
        name="apply_one",
    )(w_high, w_low, field, own_part, aux, aux, from_below, from_above)

    from_below = shift(pay_up, 1)
    from_above = shift(pay_down, -1)
    image2, dots = pl.pallas_call(
        functools.partial(apply_kernel, False, peers),
        out_shape=(shape((tall, nodes)), shape((peers * 8, LANES))),
        in_specs=vmem(10),
        out_specs=tuple(vmem(2)),
        scratch_shapes=[pltpu.VMEM((tall * 8, LANES), F32)] * 2,
        compiler_params=params,
        name="apply_two",
    )(w_high, w_low, image, flux_own, aux, coef, from_below, from_above, field, dots)

    gathered = lax.all_to_all(dots, "space", 0, 0, tiled=True)
    return pl.pallas_call(
        functools.partial(final_kernel, peers),
        out_shape=(shape((terms, nodes)), shape((terms, nodes))),
        in_specs=smem(1) + vmem(4),
        out_specs=tuple(vmem(2)),
        scratch_shapes=[pltpu.SMEM((2 * blocks,), jnp.int32), pltpu.VMEM((2, tall, nodes), F32)],
        compiler_params=params,
        name="finish",
    )(send_list, gathered, field, image, image2)


def solution(mesh):
    return jax.shard_map(
        shards,
        mesh=mesh,
        in_specs=(
            P(None, ("grp", "space")),
            P(("grp", "space")),
            P(("grp", "space"), None, None),
            P(None, ("grp", "space")),
            P(("grp", "space"), None),
            P(("grp", "space"), None, None),
        ),
        out_specs=(P(None, ("grp", "space")), P(None, ("grp", "space"))),
        check_vma=False,
    )
```

```python
import functools
import math

import jax
import jax.numpy as jnp
from jax import lax
from jax.experimental import pallas as pl
from jax.experimental.pallas import tpu as pltpu
from jax.sharding import PartitionSpec as P

VARS = 8
ORDER = 3
LANES = 128
SPREAD = 0.14
F32 = jnp.float32
BF16 = jnp.bfloat16


@functools.cache
def chaos_links():
    entries = []

    def grow(prefix, budget_left):
        if len(prefix) == VARS:
            entries.append(tuple(prefix))
            return
        for degree in range(budget_left + 1):
            grow(prefix + [degree], budget_left - degree)

    grow([], ORDER)
    entries.sort(key=lambda beta: (sum(beta), tuple(-v for v in beta)))
    lookup = {beta: place for place, beta in enumerate(entries)}
    links = []
    for beta in entries:
        mine = []
        for k in range(VARS):
            if beta[k] > 0:
                lowered = beta[:k] + (beta[k] - 1,) + beta[k + 1 :]
                mine.append((k, lookup[lowered], beta[k]))
            raised = beta[:k] + (beta[k] + 1,) + beta[k + 1 :]
            if raised in lookup:
                mine.append((k, lookup[raised], beta[k] + 1))
        links.append(mine)
    return links


def split(value):
    high = value.astype(BF16)
    return high, (value - high.astype(F32)).astype(BF16)


def product(high, low, w_high, w_low, dims):
    rows = high.shape[0]
    both = jnp.concatenate([high, low], axis=0)
    dot = functools.partial(lax.dot_general, dimension_numbers=(dims, ((), ())), preferred_element_type=F32)
    main = dot(both, w_high)
    return main[:rows] + (main[rows:] + dot(high, w_low))


def couple(source, target, coefs):
    first = coefs[0]
    scaled = {}
    for k in range(VARS):
        for square in range(1, ORDER + 1):
            scaled[k, square] = coefs[k + 1] if square == 1 else coefs[k + 1] * math.sqrt(square)
    for term, mine in enumerate(chaos_links()):
        total = source[term * 8 : term * 8 + 8, :]
        if first is not None:
            total = total * first
        for k, other, square in mine:
            total = total + scaled[k, square] * source[other * 8 : other * 8 + 8, :]
        target[term * 8 : term * 8 + 8, :] = total


def spread_rows(target, chunk, value):
    target[pl.ds(chunk, value.shape[0], stride=8), :] = value


def lane_iota(shape):
    return lax.broadcasted_iota(jnp.int32, shape, len(shape) - 1)


def row_iota(shape):
    return lax.broadcasted_iota(jnp.int32, shape, 0)


def pick_block(ref, place, half, rows):
    tile = ref[0:rows, pl.ds(pl.multiple_of((place // 2) * LANES, LANES), LANES)]
    return jnp.where(place % 2 == half, tile, pltpu.roll(tile, LANES // 2, 1))


def permute_blocks(ref, places, chunk, rows):
    left = pick_block(ref, places[2 * chunk], 0, rows)
    right = pick_block(ref, places[2 * chunk + 1], 1, rows)
    return jnp.where(lane_iota(left.shape) < LANES // 2, left, right)


def build_kernel(
    sends_in, cols_in, field_in, cap_in, var_in, base,
    w_high, w_low, field_p, pay_up, pay_down, own_part, aux,
    buf, turned, acc, dense, major, coupled_major, coef_major, sends, cols, field, cap, var, place, sems,
):
    blocks, slots, flat = base.shape
    terms, nodes = field.shape
    small = [
        pltpu.make_async_copy(source, target, sems.at[blocks + i])
        for i, (source, target) in enumerate(
            ((sends_in, sends), (cols_in, cols), (field_in, field), (cap_in, cap.at[0]), (var_in, var))
        )
    ]
    for copy in small:
        copy.start()
    copies = [pltpu.make_async_copy(base.at[j], buf.at[j], sems.at[j]) for j in range(blocks)]
    for copy in copies:
        copy.start()
    for copy in small:
        copy.wait()
    tall = field_p.shape[0]
    width = nodes // blocks
    steps = flat // LANES
    chunks = nodes // LANES
    order = [sends[0, j // (blocks // 2), j % (blocks // 2)] for j in range(blocks)]
    for j in range(2 * blocks):
        place[j] = j
    for j in range(blocks):
        place[order[j]] = j

    aux[...] = jnp.zeros_like(aux)
    for chunk in range(chunks):
        lanes = slice(chunk * LANES, (chunk + 1) * LANES)
        piece = permute_blocks(field, order, chunk, terms)
        field_p[0:terms, lanes] = piece
        field_p[terms:tall, lanes] = jnp.zeros((tall - terms, LANES), F32)
        spread_rows(major, chunk, field_p[:, lanes])
        weights = permute_blocks(var, order, chunk, VARS) * SPREAD
        aux[0:VARS, lanes] = weights
        aux[VARS : VARS + 1, lanes] = permute_blocks(cap, order, chunk, 1)
        spread_rows(coef_major, chunk, weights)
    coefs = [None] + [coef_major[k * 8 : k * 8 + 8, :] for k in range(VARS)]
    couple(major, coupled_major, coefs)

    for one in acc:
        one[...] = jnp.zeros_like(one)
    for j in range(blocks):
        copies[j].wait()
    for j in range(blocks):
        for step in range(steps):
            turned[j, pl.ds(step, slots, stride=steps), :] = buf[order[j], :, step * LANES : (step + 1) * LANES]
    for slot in range(slots):
        for j in range(blocks):
            where = j if slot == 0 else place[cols[order[j], slot - 1]]
            acc[j][where] += turned[j, slot * steps : (slot + 1) * steps, :]
    for j in range(blocks):
        for pair in range(blocks):
            even, odd = acc[j][2 * pair], acc[j][2 * pair + 1]
            near = lane_iota(even.shape) < width
            start = pair * nodes + j * width
            dense[pl.ds(start, steps, stride=2), :] = jnp.where(near, even, pltpu.roll(odd, width, 1))
            dense[pl.ds(start + 1, steps, stride=2), :] = jnp.where(near, pltpu.roll(even, width, 1), odd)
    for pair in range(blocks):
        lanes = slice(pair * LANES, (pair + 1) * LANES)
        w_high[:, lanes], w_low[:, lanes] = split(dense[pair * nodes : (pair + 1) * nodes, :])
    high, low = w_high[...], w_low[...]

    rows = []
    for chunk in range(chunks):
        piece = coupled_major[pl.ds(chunk, tall, stride=8), :]
        where = row_iota(piece.shape)
        rows.append(jnp.where(where < terms, piece, jnp.where(where == terms, 1.0, 0.0)))
    left = jnp.concatenate([jnp.concatenate(rows, axis=1), aux[0:VARS, :]], axis=0)
    left_high, left_low = split(left)
    flux = product(left_high, left_low, high, low, ((1,), (0,)))
    own_part[...] = flux[:, 0:nodes]
    outer = flux[:, nodes:]
    near = lane_iota((outer.shape[0], nodes)) < nodes // 2
    grown = jnp.concatenate([field_p[...], jnp.zeros((outer.shape[0] - tall, nodes), F32)], axis=0)
    where = row_iota(outer.shape)
    grown = jnp.where(where < terms, grown, 0.0)
    transfer = where >= terms
    pay_up[...] = jnp.where(near, grown, outer)
    pay_down[...] = jnp.where(near, outer, grown)


def apply_kernel(
    first, peers,
    w_high, w_low, field, own_part, aux, coef_in, from_below, from_above, *refs,
):
    if first:
        image, flux_own, pay_up, pay_down, coef_out, dots, major, result, single = refs
    else:
        field0, dots_in, image, dots, major, result = refs
    tall, nodes = field.shape
    terms = len(chaos_links())
    chunks = nodes // LANES
    below, above = from_below[0:tall, :], from_above[0:tall, :]
    near = lane_iota(below.shape) < nodes // 2
    where = row_iota(below.shape)
    halo = jnp.where(near, below, above)
    inward = jnp.where(near, above, below)
    value = field[...]
    extended = jnp.concatenate([value, halo], axis=1)
    marked = jnp.where(row_iota(extended.shape) < terms, extended, jnp.where(row_iota(extended.shape) == terms, 1.0, 0.0))
    ext_high, ext_low = split(marked)
    mixed = product(ext_high, ext_low, w_high[...], w_low[...], ((1,), (1,)))
    outflow = mixed[terms : terms + 1, :] * value - mixed

    if first:
        ones = jnp.ones((1, LANES), F32)
        wide = lane_iota((1, nodes)) < nodes // 2
        total0 = own_part[terms : terms + 1, :] + jnp.where(
            wide, from_above[terms : terms + 1, :], from_below[terms : terms + 1, :]
        )
        wide = lane_iota((VARS, nodes)) < nodes // 2
        totals = own_part[tall : tall + VARS, :] + jnp.where(
            wide, from_above[tall : tall + VARS, :], from_below[tall : tall + VARS, :]
        )
        coef = coef_out
        coef[...] = jnp.zeros_like(coef)
        for chunk in range(chunks):
            lanes = slice(chunk * LANES, (chunk + 1) * LANES)
            coef[chunk : chunk + 1, :] = ones
            coef[chunks + chunk : chunks + chunk + 1, :] = total0[:, lanes]
            coef[pl.ds(8 + chunk, VARS, stride=8), :] = aux[0:VARS, lanes]
            coef[pl.ds(8 + chunks + chunk, VARS, stride=8), :] = totals[:, lanes]
    else:
        coef = coef_in
    for chunk in range(chunks):
        lanes = slice(chunk * LANES, (chunk + 1) * LANES)
        spread_rows(major, chunk, outflow[:, lanes])
        spread_rows(major, chunks + chunk, value[:, lanes])
    couple(major, result, [coef[k * 8 : k * 8 + 8, :] for k in range(VARS + 1)])
    pieces = []
    for chunk in range(chunks):
        pieces.append(
            result[pl.ds(chunk, tall, stride=8), :] + result[pl.ds(chunks + chunk, tall, stride=8), :]
        )
    out = aux[VARS : VARS + 1, :] * value + jnp.concatenate(pieces, axis=1) - (own_part[0:tall, :] + inward)
    out = jnp.where(where < terms, out, 0.0)
    image[...] = out

    def dot(a, b):
        lanes_sum = jnp.sum(a * b, axis=0, keepdims=True)
        total = lanes_sum[:, 0:LANES]
        for chunk in range(1, chunks):
            total = total + lanes_sum[:, chunk * LANES : (chunk + 1) * LANES]
        return total

    if first:
        dots[...] = jnp.zeros_like(dots)
        dots[0:1, :] = dot(value, value)
        dots[1:2, :] = dot(value, out)
        dots[2:3, :] = dot(out, out)
        for chunk in range(chunks):
            spread_rows(single, chunk, out[:, chunk * LANES : (chunk + 1) * LANES])
        couple(single, result, [None] + [coef[k * 8 + 8 : k * 8 + 16, :] for k in range(VARS)])
        rows = []
        for chunk in range(chunks):
            piece = result[pl.ds(chunk, tall, stride=8), :]
            rows.append(jnp.where(row_iota(piece.shape) < terms, piece, 0.0))
        c_high, c_low = split(jnp.concatenate(rows, axis=1))
        flux = product(c_high, c_low, w_high[...], w_low[...], ((1,), (0,)))
        flux_own[...] = flux[:, 0:nodes]
        outer = flux[:, nodes:]
        pay_up[...] = jnp.where(near, out, outer)
        pay_down[...] = jnp.where(near, outer, out)
    else:
        all_dots = dots_in[...]
        row = row_iota(all_dots.shape)
        all_dots = jnp.where(row == 3, dot(field0[...], out), all_dots)
        all_dots = jnp.where(row == 4, dot(value, out), all_dots)
        for peer in range(peers):
            dots[peer * 8 : peer * 8 + 8, :] = all_dots


def final_kernel(peers, sends, dots, field, image, image2, solution_out, residual_out, place, work):
    terms, nodes = solution_out.shape
    halves = sends.shape[2]
    blocks = 2 * halves
    chunks = nodes // LANES
    for j in range(blocks):
        place[sends[0, j // halves, j % halves]] = j
    places = [place[j] for j in range(blocks)]
    total = dots[0:8, :]
    for peer in range(1, peers):
        total = total + dots[peer * 8 : peer * 8 + 8, :]

    def add(row):
        return jnp.sum(row, axis=1, keepdims=True)

    bb, by, yy, bz, yz = (total[k : k + 1, :] for k in range(5))
    norm = add(bb)
    step0 = norm / add(by)
    norm1 = add(bb - step0 * (2.0 * by - step0 * yy))
    ratio = norm1 / norm
    grow = 1.0 + ratio
    curve = add(grow * grow * by - step0 * (grow * (bz + yy) - step0 * yz))
    step1 = norm1 / curve
    c1 = step0 + step1 * grow
    c2 = step0 * step1
    work[0] = c1 * field[...] - c2 * image[...]
    work[1] = field[...] - c1 * image[...] + c2 * image2[...]
    for which, out in enumerate((solution_out, residual_out)):
        for chunk in range(chunks):
            out[:, chunk * LANES : (chunk + 1) * LANES] = permute_blocks(work.at[which], places, chunk, terms)


def vmem(count):
    return [pl.BlockSpec(memory_space=pltpu.VMEM)] * count


def smem(count):
    return [pl.BlockSpec(memory_space=pltpu.SMEM)] * count


def in_hbm(value):
    return pltpu.with_memory_space_constraint(value, pltpu.HBM)


def shape(dims, dtype=F32):
    return jax.ShapeDtypeStruct(dims, dtype)


def shift(value, steps):
    count = lax.axis_size("space")
    pairs = [(i, (i + steps) % count) for i in range(count)]
    return lax.ppermute(value, "space", pairs)


def shards(right_side, capacity, base_cond, var_field, block_cols, send_list):
    blocks, slots, flat = base_cond.shape
    terms, nodes = right_side.shape
    peers = lax.axis_size("space")
    tall = -(-terms // 8) * 8
    steps = flat // LANES
    params = pltpu.CompilerParams(vmem_limit_bytes=48 * 1024 * 1024)

    w_high, w_low, field, pay_up, pay_down, own_part, aux = pl.pallas_call(
        build_kernel,
        out_shape=(
            shape((nodes, 2 * nodes), BF16),
            shape((nodes, 2 * nodes), BF16),
            shape((tall, nodes)),
            shape((tall + VARS, nodes)),
            shape((tall + VARS, nodes)),
            shape((tall + VARS, nodes)),
            shape((2 * VARS, nodes)),
        ),
        in_specs=[pl.BlockSpec(memory_space=pltpu.HBM)] * 6,
        out_specs=tuple(vmem(7)),
        scratch_shapes=[
            pltpu.VMEM((blocks, slots, flat), F32),
            pltpu.VMEM((blocks, slots * steps, LANES), F32),
            [pltpu.VMEM((2 * blocks, steps, LANES), F32) for _ in range(blocks)],
            pltpu.VMEM((blocks * nodes, LANES), F32),
            pltpu.VMEM((tall * 8, LANES), F32),
            pltpu.VMEM((tall * 8, LANES), F32),
            pltpu.VMEM((VARS * 8, LANES), F32),
            pltpu.SMEM(send_list.shape, jnp.int32),
            pltpu.SMEM(block_cols.shape, jnp.int32),
            pltpu.VMEM((terms, nodes), F32),
            pltpu.VMEM((1, nodes), F32),
            pltpu.VMEM((VARS, nodes), F32),
            pltpu.SMEM((2 * blocks,), jnp.int32),
            pltpu.SemaphoreType.DMA((blocks + 5,)),
        ],
        compiler_params=params,
        name="build",
    )(*(in_hbm(x) for x in (send_list, block_cols, right_side, capacity, var_field, base_cond)))

    from_below = shift(pay_up, 1)
    from_above = shift(pay_down, -1)
    image, flux_own, pay_up, pay_down, coef, dots = pl.pallas_call(
        functools.partial(apply_kernel, True, peers),
        out_shape=(
            shape((tall, nodes)),
            shape((tall, nodes)),
            shape((tall, nodes)),
            shape((tall, nodes)),
            shape((8 * (VARS + 1), LANES)),
            shape((8, LANES)),
        ),
        in_specs=vmem(8),
        out_specs=tuple(vmem(6)),
        scratch_shapes=[pltpu.VMEM((tall * 8, LANES), F32)] * 3,
        compiler_params=params,
        name="apply_one",
    )(w_high, w_low, field, own_part, aux, aux, from_below, from_above)

    from_below = shift(pay_up, 1)
    from_above = shift(pay_down, -1)
    image2, dots = pl.pallas_call(
        functools.partial(apply_kernel, False, peers),
        out_shape=(shape((tall, nodes)), shape((peers * 8, LANES))),
        in_specs=vmem(10),
        out_specs=tuple(vmem(2)),
        scratch_shapes=[pltpu.VMEM((tall * 8, LANES), F32)] * 2,
        compiler_params=params,
        name="apply_two",
    )(w_high, w_low, image, flux_own, aux, coef, from_below, from_above, field, dots)

    gathered = lax.all_to_all(dots, "space", 0, 0, tiled=True)
    return pl.pallas_call(
        functools.partial(final_kernel, peers),
        out_shape=(shape((terms, nodes)), shape((terms, nodes))),
        in_specs=smem(1) + vmem(4),
        out_specs=tuple(vmem(2)),
        scratch_shapes=[pltpu.SMEM((2 * blocks,), jnp.int32), pltpu.VMEM((2, tall, nodes), F32)],
        compiler_params=params,
        name="finish",
    )(send_list, gathered, field, image, image2)


def solution(mesh):
    return jax.shard_map(
        shards,
        mesh=mesh,
        in_specs=(
            P(None, ("grp", "space")),
            P(("grp", "space")),
            P(("grp", "space"), None, None),
            P(None, ("grp", "space")),
            P(("grp", "space"), None),
            P(("grp", "space"), None, None),
        ),
        out_specs=(P(None, ("grp", "space")), P(None, ("grp", "space"))),
        check_vma=False,
    )
```

```python
import functools
import math

import jax
import jax.numpy as jnp
from jax import lax
from jax.experimental import pallas as pl
from jax.experimental.pallas import tpu as pltpu
from jax.sharding import PartitionSpec as P

VARS = 8
ORDER = 3
LANES = 128
SPREAD = 0.14
F32 = jnp.float32
BF16 = jnp.bfloat16


@functools.cache
def chaos_links():
    entries = []

    def grow(prefix, budget_left):
        if len(prefix) == VARS:
            entries.append(tuple(prefix))
            return
        for degree in range(budget_left + 1):
            grow(prefix + [degree], budget_left - degree)

    grow([], ORDER)
    entries.sort(key=lambda beta: (sum(beta), tuple(-v for v in beta)))
    lookup = {beta: place for place, beta in enumerate(entries)}
    links = []
    for beta in entries:
        mine = []
        for k in range(VARS):
            if beta[k] > 0:
                lowered = beta[:k] + (beta[k] - 1,) + beta[k + 1 :]
                mine.append((k, lookup[lowered], beta[k]))
            raised = beta[:k] + (beta[k] + 1,) + beta[k + 1 :]
            if raised in lookup:
                mine.append((k, lookup[raised], beta[k] + 1))
        links.append(mine)
    return links


def split(value):
    high = value.astype(BF16)
    return high, (value - high.astype(F32)).astype(BF16)


def product(high, low, w_high, w_low, dims):
    rows = high.shape[0]
    both = jnp.concatenate([high, low], axis=0)
    dot = functools.partial(lax.dot_general, dimension_numbers=(dims, ((), ())), preferred_element_type=F32)
    main = dot(both, w_high)
    return main[:rows] + (main[rows:] + dot(high, w_low))


def couple(source, target, coefs):
    first = coefs[0]
    scaled = {}
    for k in range(VARS):
        for square in range(1, ORDER + 1):
            scaled[k, square] = coefs[k + 1] if square == 1 else coefs[k + 1] * math.sqrt(square)
    for term, mine in enumerate(chaos_links()):
        total = source[term * 8 : term * 8 + 8, :]
        if first is not None:
            total = total * first
        for k, other, square in mine:
            total = total + scaled[k, square] * source[other * 8 : other * 8 + 8, :]
        target[term * 8 : term * 8 + 8, :] = total


def spread_rows(target, chunk, value):
    target[pl.ds(chunk, value.shape[0], stride=8), :] = value


def lane_iota(shape):
    return lax.broadcasted_iota(jnp.int32, shape, len(shape) - 1)


def row_iota(shape):
    return lax.broadcasted_iota(jnp.int32, shape, 0)


def pick_block(ref, place, half, rows):
    tile = ref[0:rows, pl.ds(pl.multiple_of((place // 2) * LANES, LANES), LANES)]
    return jnp.where(place % 2 == half, tile, pltpu.roll(tile, LANES // 2, 1))


def permute_blocks(ref, places, chunk, rows):
    left = pick_block(ref, places[2 * chunk], 0, rows)
    right = pick_block(ref, places[2 * chunk + 1], 1, rows)
    return jnp.where(lane_iota(left.shape) < LANES // 2, left, right)


def marked(value, terms):
    row = row_iota(value.shape)
    return jnp.where(row < terms, value, jnp.where(row == terms, 1.0, 0.0))


def lower_half(value):
    return lane_iota(value.shape) < value.shape[1] // 2


def by_side(near, far):
    place, count = lax.axis_index("space"), lax.axis_size("space")
    far = jnp.where((place == 0) | (place == count - 1), 0.0, far)
    even = place % 2 == 0
    return jnp.where(even, far, near), jnp.where(even, near, far)


def store_sides(near, far, up, down):
    even = lax.axis_index("space") % 2 == 0
    near[...] = jnp.where(even, up, down)
    far[...] = jnp.where(even, down, up)


def gather_chunks(ref, first, chunks, tall):
    return jnp.concatenate([ref[pl.ds(first + chunk, tall, stride=8), :] for chunk in range(chunks)], axis=1)


def scatter_chunks(ref, first, value):
    for chunk in range(value.shape[1] // LANES):
        spread_rows(ref, first + chunk, value[:, chunk * LANES : (chunk + 1) * LANES])


def coef_list(ref):
    return [ref[k * 8 : k * 8 + 8, :] for k in range(VARS + 1)]


def set_coefs(ref, first, leading, rest):
    for chunk in range(leading.shape[1] // LANES):
        lanes = slice(chunk * LANES, (chunk + 1) * LANES)
        ref[first + chunk : first + chunk + 1, :] = leading[:, lanes]
        ref[pl.ds(8 + first + chunk, VARS, stride=8), :] = rest[:, lanes]


def lane_dot(a, b):
    lanes_sum = jnp.sum(a * b, axis=0, keepdims=True)
    total = lanes_sum[:, 0:LANES]
    for start in range(LANES, a.shape[1], LANES):
        total = total + lanes_sum[:, start : start + LANES]
    return total


def order_of(sends):
    halves = sends.shape[2]
    return [sends[0, j // halves, j % halves] for j in range(2 * halves)]


def send_kernel(sends_in, field_in, field_p, near, far, sends, field, sems):
    terms, nodes = field_in.shape
    tall = field_p.shape[0]
    copies = [
        pltpu.make_async_copy(sends_in, sends, sems.at[0]),
        pltpu.make_async_copy(field_in, field, sems.at[1]),
    ]
    for copy in copies:
        copy.start()
    for copy in copies:
        copy.wait()
    order = order_of(sends)
    for chunk in range(nodes // LANES):
        lanes = slice(chunk * LANES, (chunk + 1) * LANES)
        field_p[0:terms, lanes] = permute_blocks(field, order, chunk, terms)
        field_p[terms:tall, lanes] = jnp.zeros((tall - terms, LANES), F32)
    value = field_p[...]
    store_sides(near, far, value[:, : nodes - LANES], value[:, LANES:])


def build_kernel(
    sends_in, cols_in, cap_in, var_in, base, field_p,
    w_high, w_low, part, near_own, flux_out, coef_own, coef_halo, cap_p,
    buf, turned, acc, dense, major, result, weights_p, sends, cols, cap, var, place, sems,
):
    blocks, slots, flat = base.shape
    tall, nodes = field_p.shape
    terms = len(chaos_links())
    width = nodes // blocks
    steps = flat // LANES
    chunks = nodes // LANES
    small = [
        pltpu.make_async_copy(source, target, sems.at[blocks + i])
        for i, (source, target) in enumerate(
            ((sends_in, sends), (cols_in, cols), (cap_in, cap.at[0]), (var_in, var))
        )
    ]
    for copy in small:
        copy.start()
    copies = [pltpu.make_async_copy(base.at[j], buf.at[j], sems.at[j]) for j in range(blocks)]
    for copy in copies:
        copy.start()
    for copy in small:
        copy.wait()
    order = order_of(sends)
    for j in range(2 * blocks):
        place[j] = j
    for j in range(blocks):
        place[order[j]] = j

    for chunk in range(chunks):
        lanes = slice(chunk * LANES, (chunk + 1) * LANES)
        weights_p[:, lanes] = permute_blocks(var, order, chunk, VARS) * SPREAD
        cap_p[:, lanes] = permute_blocks(cap, order, chunk, 1)
    weights = weights_p[...]
    value = field_p[...]
    for coef in (coef_own, coef_halo):
        coef[...] = jnp.zeros_like(coef)
        set_coefs(coef, 0, jnp.ones((1, nodes), F32), weights)
    scatter_chunks(major, 0, value)
    couple(major, result, coef_list(coef_own))

    for one in acc:
        one[...] = jnp.zeros_like(one)
    for copy in copies:
        copy.wait()
    for j in range(blocks):
        for step in range(steps):
            turned[j, pl.ds(step, slots, stride=steps), :] = buf[order[j], :, step * LANES : (step + 1) * LANES]
    for slot in range(slots):
        for j in range(blocks):
            where = j if slot == 0 else place[cols[order[j], slot - 1]]
            acc[j][where] += turned[j, slot * steps : (slot + 1) * steps, :]
    for j in range(blocks):
        for pair in range(blocks):
            even, odd = acc[j][2 * pair], acc[j][2 * pair + 1]
            near = lane_iota(even.shape) < width
            start = pair * nodes + j * width
            dense[pl.ds(start, steps, stride=2), :] = jnp.where(near, even, pltpu.roll(odd, width, 1))
            dense[pl.ds(start + 1, steps, stride=2), :] = jnp.where(near, pltpu.roll(even, width, 1), odd)
    for pair in range(blocks):
        lanes = slice(pair * LANES, (pair + 1) * LANES)
        w_high[:, lanes], w_low[:, lanes] = split(dense[pair * nodes : (pair + 1) * nodes, :])

    left = jnp.concatenate([marked(gather_chunks(result, 0, chunks, tall), terms), weights], axis=0)
    flux = product(*split(left), w_high[...], w_low[...], ((1,), (0,)))
    for coef, first, lanes in ((coef_own, chunks, slice(0, nodes)), (coef_halo, chunks, slice(nodes, 2 * nodes))):
        set_coefs(coef, first, flux[terms : terms + 1, lanes], flux[tall : tall + VARS, lanes])
    flux_out[...] = flux[0:tall, nodes:]
    near_own[...] = product(
        *split(marked(value, terms)), w_high[:, 0:nodes], w_low[:, 0:nodes], ((1,), (1,))
    )
    scatter_chunks(major, chunks, value)
    couple(major, result, coef_list(coef_own))
    part[...] = cap_p[...] * value + gather_chunks(result, chunks, chunks, tall) - flux[0:tall, 0:nodes]


def local_kernel(
    w_high, w_low, field, part, near_own, flux_halo, coef_halo, got_near, got_far,
    local, halo_flux, near, far, major, result,
):
    tall, nodes = field.shape
    terms = len(chaos_links())
    chunks = nodes // LANES
    below, above = by_side(got_near[...], got_far[...])
    gap = jnp.zeros((tall, LANES), F32)
    halo = jnp.concatenate([below, gap], axis=1)
    halo = jnp.where(lower_half(halo), halo, jnp.concatenate([gap, above], axis=1))
    value = field[...]
    row = row_iota(value.shape)
    mixed = near_own[...] + product(
        *split(marked(halo, terms)), w_high[:, nodes:], w_low[:, nodes:], ((1,), (1,))
    )
    scatter_chunks(major, 0, mixed[terms : terms + 1, :] * value - mixed)
    scatter_chunks(major, chunks, halo)
    couple(major, result, coef_list(coef_halo))
    own = jnp.where(row < terms, part[...] + gather_chunks(result, 0, chunks, tall), 0.0)
    outer = jnp.where(row < terms, gather_chunks(result, chunks, chunks, tall) - flux_halo[...], 0.0)
    local[...] = own
    halo_flux[...] = outer
    half = lower_half(own)
    store_sides(near, far, jnp.where(half, own, outer), jnp.where(half, outer, own))


def second_kernel(
    peers,
    w_high, w_low, field, local, halo_flux, cap, coef_own, coef_halo, got_near, got_far,
    image, local2, near, far, dots, major, result, major2, result2,
):
    tall, nodes = field.shape
    terms = len(chaos_links())
    chunks = nodes // LANES
    below, above = by_side(got_near[...], got_far[...])
    half = lower_half(below)
    row = row_iota(below.shape)
    value = jnp.where(row < terms, local[...] + jnp.where(half, above, below), 0.0)
    halo = jnp.where(row < terms, halo_flux[...] + jnp.where(half, below, above), 0.0)
    image[...] = value
    scatter_chunks(major, 0, value)
    scatter_chunks(major, chunks, value)
    mixed = product(
        *split(marked(jnp.concatenate([value, halo], axis=1), terms)), w_high[...], w_low[...], ((1,), (1,))
    )
    scatter_chunks(major2, 0, mixed[terms : terms + 1, :] * value - mixed)
    scatter_chunks(major2, chunks, halo)
    couple(major, result, coef_list(coef_own))
    coupled = jnp.where(row < terms, gather_chunks(result, 0, chunks, tall), 0.0)
    flux = product(*split(coupled), w_high[...], w_low[...], ((1,), (0,)))
    couple(major2, result2, coef_list(coef_halo))
    own = cap[...] * value + gather_chunks(result, chunks, chunks, tall)
    own = own + gather_chunks(result2, 0, chunks, tall) - flux[:, 0:nodes]
    own = jnp.where(row < terms, own, 0.0)
    outer = gather_chunks(result2, chunks, chunks, tall) - flux[:, nodes:]
    outer = jnp.where(row < terms, outer, 0.0)
    local2[...] = own
    store_sides(near, far, outer[:, LANES:], outer[:, : nodes - LANES])
    rows = [
        lane_dot(field[...], field[...]),
        lane_dot(field[...], value),
        lane_dot(value, value),
        lane_dot(value, own) + lane_dot(halo, outer),
        jnp.zeros((4, LANES), F32),
    ]
    rows = jnp.concatenate(rows, axis=0)
    for peer in range(peers):
        dots[peer * 8 : peer * 8 + 8, :] = rows


def final_kernel(
    peers, sends, dots, field, image, local2, got_near, got_far,
    solution_out, residual_out, place, work, out, sems,
):
    terms, nodes = solution_out.shape
    tall = field.shape[0]
    order = order_of(sends)
    blocks = len(order)
    for j in range(blocks):
        place[order[j]] = j
    places = [place[j] for j in range(blocks)]
    total = dots[0:8, :]
    for peer in range(1, peers):
        total = total + dots[peer * 8 : peer * 8 + 8, :]

    def add(row):
        return jnp.sum(row, axis=1, keepdims=True)

    bb, by, yy, yz = (total[k : k + 1, :] for k in range(4))
    norm = add(bb)
    step0 = norm / add(by)
    norm1 = add(bb - step0 * (2.0 * by - step0 * yy))
    ratio = norm1 / norm
    grow = 1.0 + ratio
    curve = add(grow * grow * by - step0 * (grow * (2.0 * yy) - step0 * yz))
    step1 = norm1 / curve
    c1 = step0 + step1 * grow
    c2 = step0 * step1
    work[0] = c1 * field[...] - c2 * image[...]
    below, above = by_side(got_near[...], got_far[...])
    gap = jnp.zeros((tall, LANES), F32)
    inward = jnp.concatenate([above, gap], axis=1)
    inward = jnp.where(lower_half(inward), inward, jnp.concatenate([gap, below], axis=1))
    work[1] = field[...] - c1 * image[...] + c2 * (local2[...] + inward)
    copies = []
    for which, target in enumerate((solution_out, residual_out)):
        for chunk in range(nodes // LANES):
            lanes = slice(chunk * LANES, (chunk + 1) * LANES)
            out[which, :, lanes] = permute_blocks(work.at[which], places, chunk, terms)
        copies.append(pltpu.make_async_copy(out.at[which], target, sems.at[which]))
        copies[-1].start()
    for copy in copies:
        copy.wait()


def vmem(count):
    return [pl.BlockSpec(memory_space=pltpu.VMEM)] * count


def hbm(count):
    return [pl.BlockSpec(memory_space=pltpu.HBM)] * count


def smem(count):
    return [pl.BlockSpec(memory_space=pltpu.SMEM)] * count


def in_hbm(value):
    return pltpu.with_memory_space_constraint(value, pltpu.HBM)


def shape(dims, dtype=F32):
    return jax.ShapeDtypeStruct(dims, dtype)


def exchange(near, far):
    count, groups = lax.axis_size("space"), lax.axis_size("grp")
    outer = []
    for group in range(groups):
        start = group * count
        outer += [(start + i, start + (i + 1 if i % 2 else i - 1)) for i in range(1, count - 1)]
        mate = (group ^ 1 if groups % 2 == 0 else group) * count
        ends = (0, count - 1) if groups % 2 == 0 else (count - 1, 0)
        outer += [(start, mate + ends[0]), (start + count - 1, mate + ends[1])]
    inner = [(i, i ^ 1) for i in range(count)]
    got_far = lax.ppermute(far, ("grp", "space"), outer)
    got_near = lax.ppermute(near, "space", inner)
    return got_near, got_far


def shards(right_side, capacity, base_cond, var_field, block_cols, send_list):
    blocks, slots, flat = base_cond.shape
    terms, nodes = right_side.shape
    peers = lax.axis_size("space")
    tall = -(-terms // 8) * 8
    steps = flat // LANES
    params = pltpu.CompilerParams(vmem_limit_bytes=48 * 1024 * 1024)
    wide = shape((tall, nodes))
    piece = shape((tall, nodes - LANES))
    coefs = shape((8 * (VARS + 1), LANES))
    weights = shape((nodes, 2 * nodes), BF16)
    spread = pltpu.VMEM((tall * 8, LANES), F32)
    sends = in_hbm(send_list)

    field, near, far = pl.pallas_call(
        send_kernel,
        out_shape=(wide, piece, piece),
        in_specs=hbm(2),
        out_specs=tuple(vmem(3)),
        scratch_shapes=[
            pltpu.SMEM(send_list.shape, jnp.int32),
            pltpu.VMEM((terms, nodes), F32),
            pltpu.SemaphoreType.DMA((2,)),
        ],
        compiler_params=params,
        name="send",
    )(sends, in_hbm(right_side))
    got = exchange(near, far)

    w_high, w_low, part, near_own, flux_halo, coef_own, coef_halo, cap = pl.pallas_call(
        build_kernel,
        out_shape=(weights, weights, wide, wide, wide, coefs, coefs, shape((1, nodes))),
        in_specs=hbm(5) + vmem(1),
        out_specs=tuple(vmem(8)),
        scratch_shapes=[
            pltpu.VMEM((blocks, slots, flat), F32),
            pltpu.VMEM((blocks, slots * steps, LANES), F32),
            [pltpu.VMEM((2 * blocks, steps, LANES), F32) for _ in range(blocks)],
            pltpu.VMEM((blocks * nodes, LANES), F32),
            spread,
            spread,
            pltpu.VMEM((VARS, nodes), F32),
            pltpu.SMEM(send_list.shape, jnp.int32),
            pltpu.SMEM(block_cols.shape, jnp.int32),
            pltpu.VMEM((1, nodes), F32),
            pltpu.VMEM((VARS, nodes), F32),
            pltpu.SMEM((2 * blocks,), jnp.int32),
            pltpu.SemaphoreType.DMA((blocks + 4,)),
        ],
        compiler_params=params,
        cost_estimate=pl.CostEstimate(flops=10**9, bytes_accessed=4 * 10**6, transcendentals=0),
        name="build",
    )(sends, in_hbm(block_cols), in_hbm(capacity), in_hbm(var_field), in_hbm(base_cond), field)

    local, halo_flux, near, far = pl.pallas_call(
        local_kernel,
        out_shape=(wide, wide, wide, wide),
        in_specs=vmem(9),
        out_specs=tuple(vmem(4)),
        scratch_shapes=[spread] * 2,
        compiler_params=params,
        name="local",
    )(w_high, w_low, field, part, near_own, flux_halo, coef_halo, *got)
    got = exchange(near, far)

    image, local2, near, far, dots = pl.pallas_call(
        functools.partial(second_kernel, peers),
        out_shape=(wide, wide, piece, piece, shape((peers * 8, LANES))),
        in_specs=vmem(10),
        out_specs=tuple(vmem(5)),
        scratch_shapes=[spread] * 4,
        compiler_params=params,
        name="second",
    )(w_high, w_low, field, local, halo_flux, cap, coef_own, coef_halo, *got)
    got = exchange(near, far)
    gathered = lax.all_to_all(dots, "space", 0, 0, tiled=True)

    return pl.pallas_call(
        functools.partial(final_kernel, peers),
        out_shape=(shape((terms, nodes)), shape((terms, nodes))),
        in_specs=smem(1) + vmem(6),
        out_specs=tuple(hbm(2)),
        scratch_shapes=[
            pltpu.SMEM((2 * blocks,), jnp.int32),
            pltpu.VMEM((2, tall, nodes), F32),
            pltpu.VMEM((2, terms, nodes), F32),
            pltpu.SemaphoreType.DMA((2,)),
        ],
        compiler_params=params,
        name="finish",
    )(send_list, gathered, field, image, local2, *got)


def solution(mesh):
    return jax.shard_map(
        shards,
        mesh=mesh,
        in_specs=(
            P(None, ("grp", "space")),
            P(("grp", "space")),
            P(("grp", "space"), None, None),
            P(None, ("grp", "space")),
            P(("grp", "space"), None),
            P(("grp", "space"), None, None),
        ),
        out_specs=(P(None, ("grp", "space")), P(None, ("grp", "space"))),
        check_vma=False,
    )
```

```python
import functools
import math

import jax
import jax.numpy as jnp
from jax import lax
from jax.experimental import pallas as pl
from jax.experimental.pallas import tpu as pltpu
from jax.sharding import PartitionSpec as P

VARS = 8
ORDER = 3
LANES = 128
SPREAD = 0.14
F32 = jnp.float32
BF16 = jnp.bfloat16


@functools.cache
def chaos_links():
    entries = []

    def grow(prefix, budget_left):
        if len(prefix) == VARS:
            entries.append(tuple(prefix))
            return
        for degree in range(budget_left + 1):
            grow(prefix + [degree], budget_left - degree)

    grow([], ORDER)
    entries.sort(key=lambda beta: (sum(beta), tuple(-v for v in beta)))
    lookup = {beta: place for place, beta in enumerate(entries)}
    links = []
    for beta in entries:
        mine = []
        for k in range(VARS):
            if beta[k] > 0:
                lowered = beta[:k] + (beta[k] - 1,) + beta[k + 1 :]
                mine.append((k, lookup[lowered], beta[k]))
            raised = beta[:k] + (beta[k] + 1,) + beta[k + 1 :]
            if raised in lookup:
                mine.append((k, lookup[raised], beta[k] + 1))
        links.append(mine)
    return links


def split(value):
    high = value.astype(BF16)
    return high, (value - high.astype(F32)).astype(BF16)


def product(high, low, w_high, w_low, dims):
    rows = high.shape[0]
    both = jnp.concatenate([high, low], axis=0)
    dot = functools.partial(lax.dot_general, dimension_numbers=(dims, ((), ())), preferred_element_type=F32)
    main = dot(both, w_high)
    return main[:rows] + (main[rows:] + dot(high, w_low))


def couple(source, target, coefs, part=0, parts=1):
    first = coefs[0]
    scaled = {}
    for k in range(VARS):
        for square in range(1, ORDER + 1):
            scaled[k, square] = coefs[k + 1] if square == 1 else coefs[k + 1] * math.sqrt(square)
    links = chaos_links()
    for term in range(part * len(links) // parts, (part + 1) * len(links) // parts):
        mine = links[term]
        total = source[term * 8 : term * 8 + 8, :]
        if first is not None:
            total = total * first
        for k, other, square in mine:
            total = total + scaled[k, square] * source[other * 8 : other * 8 + 8, :]
        target[term * 8 : term * 8 + 8, :] = total


def spread_rows(target, chunk, value):
    target[pl.ds(chunk, value.shape[0], stride=8), :] = value


def lane_iota(shape):
    return lax.broadcasted_iota(jnp.int32, shape, len(shape) - 1)


def row_iota(shape):
    return lax.broadcasted_iota(jnp.int32, shape, 0)


def pick_block(ref, place, half, rows):
    tile = ref[0:rows, pl.ds(pl.multiple_of((place // 2) * LANES, LANES), LANES)]
    return jnp.where(place % 2 == half, tile, pltpu.roll(tile, LANES // 2, 1))


def permute_blocks(ref, places, chunk, rows):
    left = pick_block(ref, places[2 * chunk], 0, rows)
    right = pick_block(ref, places[2 * chunk + 1], 1, rows)
    return jnp.where(lane_iota(left.shape) < LANES // 2, left, right)


def marked(value, terms):
    row = row_iota(value.shape)
    return jnp.where(row < terms, value, jnp.where(row == terms, 1.0, 0.0))


def lower_half(value):
    return lane_iota(value.shape) < value.shape[1] // 2


def by_side(near, far):
    place, count = lax.axis_index("space"), lax.axis_size("space")
    far = jnp.where((place == 0) | (place == count - 1), 0.0, far)
    even = place % 2 == 0
    return jnp.where(even, far, near), jnp.where(even, near, far)


def store_sides(near, far, up, down):
    even = lax.axis_index("space") % 2 == 0
    near[...] = jnp.where(even, up, down)
    far[...] = jnp.where(even, down, up)


def transpose8(tiles):
    tiles = [tile if t == 0 else pltpu.roll(tile, t, 0) for t, tile in enumerate(tiles)]
    row = row_iota(tiles[0].shape)
    for bit in (1, 2, 4):
        take = row & bit != 0
        tiles = [jnp.where(take, tiles[(t + bit) % 8], tiles[t]) for t in range(8)]
    return [tiles[0] if k == 0 else pltpu.roll(tiles[8 - k], 8 - k, 0) for k in range(8)]


def to_terms(target, *values):
    tiles = [(value, lane) for value in values for lane in range(0, value.shape[1], LANES)]
    for chunk, (value, lane) in enumerate(tiles):
        spread_rows(target, chunk, value[:, lane : lane + LANES])


def from_terms(source, count):
    rows = source.shape[0] // 8
    return [
        jnp.concatenate([source[pl.ds(3 * i + chunk, rows, stride=8), :] for chunk in range(3)], axis=1)
        for i in range(count)
    ]


def coef_list(ref):
    return [ref[k * 8 : k * 8 + 8, :] for k in range(VARS + 1)]


def set_coefs(ref, first, leading, rest):
    for chunk in range(leading.shape[1] // LANES):
        lanes = slice(chunk * LANES, (chunk + 1) * LANES)
        ref[first + chunk : first + chunk + 1, :] = leading[:, lanes]
        ref[pl.ds(8 + first + chunk, VARS, stride=8), :] = rest[:, lanes]


def lane_dot(a, b):
    lanes_sum = jnp.sum(a * b, axis=0, keepdims=True)
    total = lanes_sum[:, 0:LANES]
    for start in range(LANES, a.shape[1], LANES):
        total = total + lanes_sum[:, start : start + LANES]
    return total


def order_of(sends):
    halves = sends.shape[2]
    return [sends[0, j // halves, j % halves] for j in range(2 * halves)]


def send_kernel(sends_in, field_in, field_p, near, far, sends, field, sems):
    terms, nodes = field_in.shape
    tall = field_p.shape[0]
    copies = [
        pltpu.make_async_copy(sends_in, sends, sems.at[0]),
        pltpu.make_async_copy(field_in, field, sems.at[1]),
    ]
    for copy in copies:
        copy.start()
    for copy in copies:
        copy.wait()
    order = order_of(sends)
    for chunk in range(nodes // LANES):
        lanes = slice(chunk * LANES, (chunk + 1) * LANES)
        field_p[0:terms, lanes] = permute_blocks(field, order, chunk, terms)
        field_p[terms:tall, lanes] = jnp.zeros((tall - terms, LANES), F32)
    value = field_p[...]
    store_sides(near, far, value[:, : nodes - LANES], value[:, LANES:])


def build_kernel(
    sends_in, cols_in, cap_in, var_in, base, field_p,
    w_high, w_low, part, near_own, flux_out, coef_own, coef_halo, cap_p,
    buf, acc, dense, major, result, weights_p, sends, cols, cap, var, place, sems,
):
    blocks, slots, flat = base.shape
    tall, nodes = field_p.shape
    terms = len(chaos_links())
    width = nodes // blocks
    steps = flat // LANES
    chunks = nodes // LANES
    small = [
        pltpu.make_async_copy(source, target, sems.at[blocks + i])
        for i, (source, target) in enumerate(
            ((sends_in, sends), (cols_in, cols), (cap_in, cap.at[0]), (var_in, var))
        )
    ]
    for copy in small:
        copy.start()
    copies = [pltpu.make_async_copy(base.at[j], buf.at[j], sems.at[j]) for j in range(blocks)]
    for copy in copies:
        copy.start()
    for copy in small:
        copy.wait()
    order = order_of(sends)
    for j in range(2 * blocks):
        place[j] = j
    for j in range(blocks):
        place[order[j]] = j

    for chunk in range(chunks):
        lanes = slice(chunk * LANES, (chunk + 1) * LANES)
        weights_p[:, lanes] = permute_blocks(var, order, chunk, VARS) * SPREAD
        cap_p[:, lanes] = permute_blocks(cap, order, chunk, 1)
    weights = weights_p[...]
    value = field_p[...]
    for coef in (coef_own, coef_halo):
        coef[...] = jnp.zeros_like(coef)
        set_coefs(coef, 0, jnp.ones((1, nodes), F32), weights)
    to_terms(major, value, value)
    couple(major, result, coef_list(coef_own))

    for one in acc:
        one[...] = jnp.zeros_like(one)
    for copy in copies:
        copy.wait()
    for slot in range(0, slots, 8):
        for j in range(blocks):
            spots = [j if s == 0 else place[cols[order[j], s - 1]] for s in range(slot, slot + 8)]
            for step in range(0, steps, 8):
                tiles = [
                    buf[order[j], slot : slot + 8, t * LANES : (t + 1) * LANES] for t in range(step, step + 8)
                ]
                for spot, tile in zip(spots, transpose8(tiles)):
                    acc[j][spot, step : step + 8, :] += tile
    row = row_iota((8, LANES))
    near = lane_iota((8, LANES)) < width
    for j in range(blocks):
        for pair in range(blocks):
            lanes = slice(pair * LANES, (pair + 1) * LANES)
            for step in range(0, steps, 8):
                even = acc[j][2 * pair, step : step + 8, :]
                odd = acc[j][2 * pair + 1, step : step + 8, :]
                first = jnp.where(near, even, pltpu.roll(odd, width, 1))
                second = jnp.where(near, pltpu.roll(even, width, 1), odd)
                for half in range(2):
                    pick = row // 2 + 4 * half
                    start = j * width + 2 * step + 8 * half
                    dense[start : start + 8, lanes] = jnp.where(
                        row % 2 == 0,
                        jnp.take_along_axis(first, pick, axis=0),
                        jnp.take_along_axis(second, pick, axis=0),
                    )
    for pair in range(blocks):
        lanes = slice(pair * LANES, (pair + 1) * LANES)
        w_high[:, lanes], w_low[:, lanes] = split(dense[:, lanes])

    left = jnp.concatenate([marked(from_terms(result, 1)[0], terms), weights], axis=0)
    flux = product(*split(left), w_high[...], w_low[...], ((1,), (0,)))
    for coef, first, lanes in ((coef_own, chunks, slice(0, nodes)), (coef_halo, chunks, slice(nodes, 2 * nodes))):
        set_coefs(coef, first, flux[terms : terms + 1, lanes], flux[tall : tall + VARS, lanes])
    flux_out[...] = flux[0:tall, nodes:]
    near_own[...] = product(
        *split(marked(value, terms)), w_high[:, 0:nodes], w_low[:, 0:nodes], ((1,), (1,))
    )
    couple(major, result, coef_list(coef_own))
    part[...] = cap_p[...] * value + from_terms(result, 2)[1] - flux[0:tall, 0:nodes]


def local_kernel(
    w_high, w_low, field, part, near_own, flux_halo, coef_halo, got_near, got_far,
    local, halo_flux, near, far, major, result,
):
    tall, nodes = field.shape
    terms = len(chaos_links())
    below, above = by_side(got_near[...], got_far[...])
    gap = jnp.zeros((tall, LANES), F32)
    halo = jnp.concatenate([below, gap], axis=1)
    halo = jnp.where(lower_half(halo), halo, jnp.concatenate([gap, above], axis=1))
    value = field[...]
    row = row_iota(value.shape)
    mixed = near_own[...] + product(
        *split(marked(halo, terms)), w_high[:, nodes:], w_low[:, nodes:], ((1,), (1,))
    )
    to_terms(major, mixed[terms : terms + 1, :] * value - mixed, halo)
    couple(major, result, coef_list(coef_halo))
    forward, outer = from_terms(result, 2)
    own = jnp.where(row < terms, part[...] + forward, 0.0)
    outer = jnp.where(row < terms, outer - flux_halo[...], 0.0)
    local[...] = own
    halo_flux[...] = outer
    half = lower_half(own)
    store_sides(near, far, jnp.where(half, own, outer), jnp.where(half, outer, own))


def second_kernel(
    peers,
    w_high, w_low, field, local, halo_flux, cap, coef_own, coef_halo, got_near, got_far,
    image, local2, near, far, dots, major, result, major2, result2,
):
    _, nodes = field.shape
    terms = len(chaos_links())
    below, above = by_side(got_near[...], got_far[...])
    half = lower_half(below)
    row = row_iota(below.shape)
    value = jnp.where(row < terms, local[...] + jnp.where(half, above, below), 0.0)
    halo = jnp.where(row < terms, halo_flux[...] + jnp.where(half, below, above), 0.0)
    image[...] = value
    to_terms(major, value, value)
    extended = split(marked(jnp.concatenate([value, halo], axis=1), terms))
    coefs = coef_list(coef_own)
    mixed = []
    cuts = list(range(0, nodes, 2 * LANES))
    for part, start in enumerate(cuts):
        span = slice(start, min(start + 2 * LANES, nodes))
        mixed.append(product(*extended, w_high[span, :], w_low[span, :], ((1,), (1,))))
        couple(major, result, coefs, part, len(cuts))
    mixed = jnp.concatenate(mixed, axis=1)
    to_terms(major2, mixed[terms : terms + 1, :] * value - mixed, halo)
    coupled, transferred = from_terms(result, 2)
    coupled = split(jnp.where(row < terms, coupled, 0.0))
    coefs = coef_list(coef_halo)
    flux = []
    cuts = list(range(0, 2 * nodes, 2 * LANES))
    for part, start in enumerate(cuts):
        span = slice(start, start + 2 * LANES)
        flux.append(product(*coupled, w_high[:, span], w_low[:, span], ((1,), (0,))))
        couple(major2, result2, coefs, part, len(cuts))
    flux = jnp.concatenate(flux, axis=1)
    forward, outer = from_terms(result2, 2)
    own = cap[...] * value + transferred + forward - flux[:, 0:nodes]
    own = jnp.where(row < terms, own, 0.0)
    outer = outer - flux[:, nodes:]
    outer = jnp.where(row < terms, outer, 0.0)
    local2[...] = own
    store_sides(near, far, outer[:, LANES:], outer[:, : nodes - LANES])
    sums = [
        lane_dot(field[...], field[...]),
        lane_dot(field[...], value),
        lane_dot(value, value),
        lane_dot(value, own) + lane_dot(halo, outer),
    ]
    lane = lane_iota((1, LANES))
    packed = jnp.zeros((1, LANES), F32)
    for k, one in enumerate(sums):
        one = one + pltpu.roll(one, LANES // 2, 1)
        one = one + pltpu.roll(one, LANES // 4, 1)
        packed = jnp.where(lane // (LANES // 4) == k, one, packed)
    for peer in range(peers):
        dots[peer] = packed


def final_kernel(
    peers, sends, dots, field, image, local2, got_near, got_far,
    solution_out, residual_out, place, work, out, sems,
):
    terms, nodes = solution_out.shape
    tall = field.shape[0]
    order = order_of(sends)
    blocks = len(order)
    for j in range(blocks):
        place[order[j]] = j
    places = [place[j] for j in range(blocks)]
    total = dots[0]
    for peer in range(1, peers):
        total = total + dots[peer]
    quarter = lane_iota(total.shape) < LANES // 4

    def add(row):
        return jnp.sum(jnp.where(quarter, row, 0.0), axis=1, keepdims=True)

    bb, by, yy, yz = [total] + [pltpu.roll(total, LANES - k * LANES // 4, 1) for k in range(1, 4)]
    norm = add(bb)
    step0 = norm / add(by)
    norm1 = add(bb - step0 * (2.0 * by - step0 * yy))
    ratio = norm1 / norm
    grow = 1.0 + ratio
    curve = add(grow * grow * by - step0 * (grow * (2.0 * yy) - step0 * yz))
    step1 = norm1 / curve
    c1 = step0 + step1 * grow
    c2 = step0 * step1
    copies = []

    def put(which, target):
        for chunk in range(nodes // LANES):
            lanes = slice(chunk * LANES, (chunk + 1) * LANES)
            out[which, :, lanes] = permute_blocks(work.at[which], places, chunk, terms)
        copies.append(pltpu.make_async_copy(out.at[which], target, sems.at[which]))
        copies[-1].start()

    work[0] = c1 * field[...] - c2 * image[...]
    put(0, solution_out)
    below, above = by_side(got_near[...], got_far[...])
    gap = jnp.zeros((tall, LANES), F32)
    inward = jnp.concatenate([above, gap], axis=1)
    inward = jnp.where(lower_half(inward), inward, jnp.concatenate([gap, below], axis=1))
    work[1] = field[...] - c1 * image[...] + c2 * (local2[...] + inward)
    put(1, residual_out)
    for copy in copies:
        copy.wait()


def vmem(count):
    return [pl.BlockSpec(memory_space=pltpu.VMEM)] * count


def hbm(count):
    return [pl.BlockSpec(memory_space=pltpu.HBM)] * count


def smem(count):
    return [pl.BlockSpec(memory_space=pltpu.SMEM)] * count


def in_hbm(value):
    return pltpu.with_memory_space_constraint(value, pltpu.HBM)


def shape(dims, dtype=F32):
    return jax.ShapeDtypeStruct(dims, dtype)


def exchange(near, far):
    count, groups = lax.axis_size("space"), lax.axis_size("grp")
    outer = []
    for group in range(groups):
        start = group * count
        outer += [(start + i, start + (i + 1 if i % 2 else i - 1)) for i in range(1, count - 1)]
        mate = (group ^ 1 if groups % 2 == 0 else group) * count
        ends = (0, count - 1) if groups % 2 == 0 else (count - 1, 0)
        outer += [(start, mate + ends[0]), (start + count - 1, mate + ends[1])]
    inner = [(i, i ^ 1) for i in range(count)]
    got_far = lax.ppermute(far, ("grp", "space"), outer)
    got_near = lax.ppermute(near, "space", inner)
    return got_near, got_far


def shards(right_side, capacity, base_cond, var_field, block_cols, send_list):
    blocks, slots, flat = base_cond.shape
    terms, nodes = right_side.shape
    peers = lax.axis_size("space")
    tall = -(-terms // 8) * 8
    steps = flat // LANES
    params = pltpu.CompilerParams(vmem_limit_bytes=48 * 1024 * 1024)
    wide = shape((tall, nodes))
    piece = shape((tall, nodes - LANES))
    coefs = shape((8 * (VARS + 1), LANES))
    weights = shape((nodes, 2 * nodes), BF16)
    spread = pltpu.VMEM((tall * 8, LANES), F32)
    sends = in_hbm(send_list)

    field, near, far = pl.pallas_call(
        send_kernel,
        out_shape=(wide, piece, piece),
        in_specs=hbm(2),
        out_specs=tuple(vmem(3)),
        scratch_shapes=[
            pltpu.SMEM(send_list.shape, jnp.int32),
            pltpu.VMEM((terms, nodes), F32),
            pltpu.SemaphoreType.DMA((2,)),
        ],
        compiler_params=params,
        name="send",
    )(sends, in_hbm(right_side))
    got = exchange(near, far)

    w_high, w_low, part, near_own, flux_halo, coef_own, coef_halo, cap = pl.pallas_call(
        build_kernel,
        out_shape=(weights, weights, wide, wide, wide, coefs, coefs, shape((1, nodes))),
        in_specs=hbm(5) + vmem(1),
        out_specs=tuple(vmem(8)),
        scratch_shapes=[
            pltpu.VMEM((blocks, slots, flat), F32),
            [pltpu.VMEM((2 * blocks, steps, LANES), F32) for _ in range(blocks)],
            pltpu.VMEM((nodes, 2 * nodes), F32),
            spread,
            spread,
            pltpu.VMEM((VARS, nodes), F32),
            pltpu.SMEM(send_list.shape, jnp.int32),
            pltpu.SMEM(block_cols.shape, jnp.int32),
            pltpu.VMEM((1, nodes), F32),
            pltpu.VMEM((VARS, nodes), F32),
            pltpu.SMEM((2 * blocks,), jnp.int32),
            pltpu.SemaphoreType.DMA((blocks + 4,)),
        ],
        compiler_params=params,
        cost_estimate=pl.CostEstimate(flops=10**9, bytes_accessed=4 * 10**6, transcendentals=0),
        name="build",
    )(sends, in_hbm(block_cols), in_hbm(capacity), in_hbm(var_field), in_hbm(base_cond), field)

    local, halo_flux, near, far = pl.pallas_call(
        local_kernel,
        out_shape=(wide, wide, wide, wide),
        in_specs=vmem(9),
        out_specs=tuple(vmem(4)),
        scratch_shapes=[spread] * 2,
        compiler_params=params,
        name="local",
    )(w_high, w_low, field, part, near_own, flux_halo, coef_halo, *got)
    got = exchange(near, far)

    image, local2, near, far, dots = pl.pallas_call(
        functools.partial(second_kernel, peers),
        out_shape=(wide, wide, piece, piece, shape((peers, 1, LANES))),
        in_specs=vmem(10),
        out_specs=tuple(vmem(5)),
        scratch_shapes=[spread] * 4,
        compiler_params=params,
        name="second",
    )(w_high, w_low, field, local, halo_flux, cap, coef_own, coef_halo, *got)
    got = exchange(near, far)
    gathered = lax.all_to_all(dots, "space", 0, 0, tiled=True)

    return pl.pallas_call(
        functools.partial(final_kernel, peers),
        out_shape=(shape((terms, nodes)), shape((terms, nodes))),
        in_specs=smem(1) + vmem(6),
        out_specs=tuple(hbm(2)),
        scratch_shapes=[
            pltpu.SMEM((2 * blocks,), jnp.int32),
            pltpu.VMEM((2, tall, nodes), F32),
            pltpu.VMEM((2, terms, nodes), F32),
            pltpu.SemaphoreType.DMA((2,)),
        ],
        compiler_params=params,
        name="finish",
    )(send_list, gathered, field, image, local2, *got)


def solution(mesh):
    return jax.shard_map(
        shards,
        mesh=mesh,
        in_specs=(
            P(None, ("grp", "space")),
            P(("grp", "space")),
            P(("grp", "space"), None, None),
            P(None, ("grp", "space")),
            P(("grp", "space"), None),
            P(("grp", "space"), None, None),
        ),
        out_specs=(P(None, ("grp", "space")), P(None, ("grp", "space"))),
        check_vma=False,
    )
```

```python
import functools
import math

import jax
import jax.numpy as jnp
from jax import lax
from jax.experimental import pallas as pl
from jax.experimental.pallas import tpu as pltpu
from jax.sharding import PartitionSpec as P

VARS = 8
ORDER = 3
LANES = 128
SPREAD = 0.14
F32 = jnp.float32
BF16 = jnp.bfloat16


@functools.cache
def chaos_links():
    entries = []

    def grow(prefix, budget_left):
        if len(prefix) == VARS:
            entries.append(tuple(prefix))
            return
        for degree in range(budget_left + 1):
            grow(prefix + [degree], budget_left - degree)

    grow([], ORDER)
    entries.sort(key=lambda beta: (sum(beta), tuple(-v for v in beta)))
    lookup = {beta: place for place, beta in enumerate(entries)}
    links = []
    for beta in entries:
        mine = []
        for k in range(VARS):
            if beta[k] > 0:
                lowered = beta[:k] + (beta[k] - 1,) + beta[k + 1 :]
                mine.append((k, lookup[lowered], beta[k]))
            raised = beta[:k] + (beta[k] + 1,) + beta[k + 1 :]
            if raised in lookup:
                mine.append((k, lookup[raised], beta[k] + 1))
        links.append(mine)
    return links


def split(value):
    high = value.astype(BF16)
    return high, (value - high.astype(F32)).astype(BF16)


def product(high, low, w_high, w_low, dims):
    rows = high.shape[0]
    both = jnp.concatenate([high, low], axis=0)
    dot = functools.partial(lax.dot_general, dimension_numbers=(dims, ((), ())), preferred_element_type=F32)
    main = dot(both, w_high)
    return main[:rows] + (main[rows:] + dot(high, w_low))


def couple(source, target, coefs, part=0, parts=1):
    first = coefs[0]
    scaled = {}
    for k in range(VARS):
        for square in range(1, ORDER + 1):
            scaled[k, square] = coefs[k + 1] if square == 1 else coefs[k + 1] * math.sqrt(square)
    links = chaos_links()
    for term in range(part * len(links) // parts, (part + 1) * len(links) // parts):
        mine = links[term]
        total = source[term * 8 : term * 8 + 8, :]
        if first is not None:
            total = total * first
        for k, other, square in mine:
            total = total + scaled[k, square] * source[other * 8 : other * 8 + 8, :]
        target[term * 8 : term * 8 + 8, :] = total


def packed_rows(tall):
    return tall + pack_fold(tall)


def pack_fold(tall):
    return (tall // 2 + 7) // 8 * 8


def pack(value, upper):
    tall = value.shape[0]
    fold = pack_fold(tall)
    middle = value[:, LANES : 2 * LANES]
    head, tail = middle[:fold], pltpu.roll(middle[tall - fold :], LANES // 2, 1)
    low = lower_half(head)
    whole = value[:, 2 * LANES :] if upper else value[:, :LANES]
    return jnp.concatenate([whole, jnp.where(low, tail, head) if upper else jnp.where(low, head, tail)], axis=0)


def unpack(lower, upper):
    tall = lower.shape[0] * 2 // 3 // 8 * 8
    while packed_rows(tall) > lower.shape[0]:
        tall -= 8
    fold = pack_fold(tall)

    def middle(got):
        bent = got[tall:]
        return jnp.concatenate([bent, pltpu.roll(bent, LANES // 2, 1)[2 * fold - tall :]], axis=0)

    first, second = middle(lower), middle(upper)
    return jnp.concatenate([lower[:tall], jnp.where(lower_half(first), first, second), upper[:tall]], axis=1)


def spread_rows(target, chunk, value):
    target[pl.ds(chunk, value.shape[0], stride=8), :] = value


def lane_iota(shape):
    return lax.broadcasted_iota(jnp.int32, shape, len(shape) - 1)


def row_iota(shape):
    return lax.broadcasted_iota(jnp.int32, shape, 0)


def pick_block(ref, place, half, rows):
    tile = ref[0:rows, pl.ds(pl.multiple_of((place // 2) * LANES, LANES), LANES)]
    return jnp.where(place % 2 == half, tile, pltpu.roll(tile, LANES // 2, 1))


def permute_blocks(ref, places, chunk, rows):
    left = pick_block(ref, places[2 * chunk], 0, rows)
    right = pick_block(ref, places[2 * chunk + 1], 1, rows)
    return jnp.where(lane_iota(left.shape) < LANES // 2, left, right)


def marked(value, terms):
    row = row_iota(value.shape)
    return jnp.where(row < terms, value, jnp.where(row == terms, 1.0, 0.0))


def lower_half(value):
    return lane_iota(value.shape) < value.shape[1] // 2


def by_side(near, far):
    place, count = lax.axis_index("space"), lax.axis_size("space")
    far = jnp.where((place == 0) | (place == count - 1), 0.0, far)
    even = place % 2 == 0
    return jnp.where(even, far, near), jnp.where(even, near, far)


def store_sides(near, far, up, down):
    even = lax.axis_index("space") % 2 == 0
    near[...] = jnp.where(even, up, down)
    far[...] = jnp.where(even, down, up)


def transpose8(tiles):
    tiles = [tile if t == 0 else pltpu.roll(tile, t, 0) for t, tile in enumerate(tiles)]
    row = row_iota(tiles[0].shape)
    for bit in (1, 2, 4):
        take = row & bit != 0
        tiles = [jnp.where(take, tiles[(t + bit) % 8], tiles[t]) for t in range(8)]
    return [tiles[0] if k == 0 else pltpu.roll(tiles[8 - k], 8 - k, 0) for k in range(8)]


def to_terms(target, *values):
    tiles = [(value, lane) for value in values for lane in range(0, value.shape[1], LANES)]
    for chunk, (value, lane) in enumerate(tiles):
        spread_rows(target, chunk, value[:, lane : lane + LANES])


def from_terms(source, count):
    rows = source.shape[0] // 8
    return [
        jnp.concatenate([source[pl.ds(3 * i + chunk, rows, stride=8), :] for chunk in range(3)], axis=1)
        for i in range(count)
    ]


def coef_list(ref):
    return [ref[k * 8 : k * 8 + 8, :] for k in range(VARS + 1)]


def set_coefs(ref, first, leading, rest):
    for chunk in range(leading.shape[1] // LANES):
        lanes = slice(chunk * LANES, (chunk + 1) * LANES)
        ref[first + chunk : first + chunk + 1, :] = leading[:, lanes]
        ref[pl.ds(8 + first + chunk, VARS, stride=8), :] = rest[:, lanes]


def lane_dot(a, b):
    lanes_sum = jnp.sum(a * b, axis=0, keepdims=True)
    total = lanes_sum[:, 0:LANES]
    for start in range(LANES, a.shape[1], LANES):
        total = total + lanes_sum[:, start : start + LANES]
    return total


def order_of(sends):
    halves = sends.shape[2]
    return [sends[0, j // halves, j % halves] for j in range(2 * halves)]


def send_kernel(sends_in, field_in, field_p, near, far, sends, field, sems):
    terms, nodes = field_in.shape
    tall = field_p.shape[0]
    copies = [
        pltpu.make_async_copy(sends_in, sends, sems.at[0]),
        pltpu.make_async_copy(field_in, field, sems.at[1]),
    ]
    for copy in copies:
        copy.start()
    for copy in copies:
        copy.wait()
    order = order_of(sends)
    for chunk in range(nodes // LANES):
        lanes = slice(chunk * LANES, (chunk + 1) * LANES)
        field_p[0:terms, lanes] = permute_blocks(field, order, chunk, terms)
        field_p[terms:tall, lanes] = jnp.zeros((tall - terms, LANES), F32)
    value = field_p[...]
    store_sides(near, far, pack(value, False), pack(value, True))


def build_kernel(
    sends_in, cols_in, cap_in, var_in, base, field_p,
    w_high, w_low, part, near_own, flux_out, coef_own, coef_halo, cap_p,
    buf, acc, dense, major, result, weights_p, sends, cols, cap, var, place, sems,
):
    blocks, slots, flat = base.shape
    tall, nodes = field_p.shape
    terms = len(chaos_links())
    width = nodes // blocks
    steps = flat // LANES
    chunks = nodes // LANES
    small = [
        pltpu.make_async_copy(source, target, sems.at[slots // 8 + i])
        for i, (source, target) in enumerate(
            ((sends_in, sends), (cols_in, cols), (cap_in, cap.at[0]), (var_in, var))
        )
    ]
    for copy in small:
        copy.start()
    copies = []
    for i in range(slots // 8):
        some = (slice(None), pl.ds(8 * i, 8))
        copies.append(pltpu.make_async_copy(base.at[some], buf.at[some], sems.at[i]))
        copies[-1].start()
    for copy in small:
        copy.wait()
    order = order_of(sends)
    for j in range(2 * blocks):
        place[j] = j
    for j in range(blocks):
        place[order[j]] = j

    for chunk in range(chunks):
        lanes = slice(chunk * LANES, (chunk + 1) * LANES)
        weights_p[:, lanes] = permute_blocks(var, order, chunk, VARS) * SPREAD
        cap_p[:, lanes] = permute_blocks(cap, order, chunk, 1)
    weights = weights_p[...]
    value = field_p[...]
    for coef in (coef_own, coef_halo):
        coef[...] = jnp.zeros_like(coef)
        set_coefs(coef, 0, jnp.ones((1, nodes), F32), weights)
    to_terms(major, value, value)
    couple(major, result, coef_list(coef_own))

    for one in acc:
        one[...] = jnp.zeros_like(one)
    for slot in range(0, slots, 8):
        copies[slot // 8].wait()
        for j in range(blocks):
            spots = [j if s == 0 else place[cols[order[j], s - 1]] for s in range(slot, slot + 8)]
            for step in range(0, steps, 8):
                tiles = [
                    buf[order[j], slot : slot + 8, t * LANES : (t + 1) * LANES] for t in range(step, step + 8)
                ]
                for spot, tile in zip(spots, transpose8(tiles)):
                    acc[j][spot, step : step + 8, :] += tile
    row = row_iota((8, LANES))
    near = lane_iota((8, LANES)) < width
    for j in range(blocks):
        for pair in range(blocks):
            lanes = slice(pair * LANES, (pair + 1) * LANES)
            for step in range(0, steps, 8):
                even = acc[j][2 * pair, step : step + 8, :]
                odd = acc[j][2 * pair + 1, step : step + 8, :]
                first = jnp.where(near, even, pltpu.roll(odd, width, 1))
                second = jnp.where(near, pltpu.roll(even, width, 1), odd)
                for half in range(2):
                    pick = row // 2 + 4 * half
                    start = j * width + 2 * step + 8 * half
                    dense[start : start + 8, lanes] = jnp.where(
                        row % 2 == 0,
                        jnp.take_along_axis(first, pick, axis=0),
                        jnp.take_along_axis(second, pick, axis=0),
                    )
    for pair in range(blocks):
        lanes = slice(pair * LANES, (pair + 1) * LANES)
        w_high[:, lanes], w_low[:, lanes] = split(dense[:, lanes])

    left = jnp.concatenate([marked(from_terms(result, 1)[0], terms), weights], axis=0)
    flux = product(*split(left), w_high[...], w_low[...], ((1,), (0,)))
    for coef, first, lanes in ((coef_own, chunks, slice(0, nodes)), (coef_halo, chunks, slice(nodes, 2 * nodes))):
        set_coefs(coef, first, flux[terms : terms + 1, lanes], flux[tall : tall + VARS, lanes])
    flux_out[...] = flux[0:tall, nodes:]
    near_own[...] = product(
        *split(marked(value, terms)), w_high[:, 0:nodes], w_low[:, 0:nodes], ((1,), (1,))
    )
    couple(major, result, coef_list(coef_own))
    part[...] = cap_p[...] * value + from_terms(result, 2)[1] - flux[0:tall, 0:nodes]


def local_kernel(
    w_high, w_low, field, part, near_own, flux_halo, coef_halo, got_near, got_far,
    local, halo_flux, near, far, major, result,
):
    _, nodes = field.shape
    terms = len(chaos_links())
    below, above = by_side(got_near[...], got_far[...])
    halo = unpack(below, above)
    value = field[...]
    row = row_iota(value.shape)
    mixed = near_own[...] + product(
        *split(marked(halo, terms)), w_high[:, nodes:], w_low[:, nodes:], ((1,), (1,))
    )
    to_terms(major, mixed[terms : terms + 1, :] * value - mixed, halo)
    couple(major, result, coef_list(coef_halo))
    forward, outer = from_terms(result, 2)
    own = jnp.where(row < terms, part[...] + forward, 0.0)
    outer = jnp.where(row < terms, outer - flux_halo[...], 0.0)
    local[...] = own
    halo_flux[...] = outer
    half = lower_half(own)
    store_sides(near, far, jnp.where(half, own, outer), jnp.where(half, outer, own))


def second_kernel(
    peers,
    w_high, w_low, field, local, halo_flux, cap, coef_own, coef_halo, got_near, got_far,
    image, local2, near, far, dots, major, result, major2, result2,
):
    _, nodes = field.shape
    terms = len(chaos_links())
    below, above = by_side(got_near[...], got_far[...])
    half = lower_half(below)
    row = row_iota(below.shape)
    value = jnp.where(row < terms, local[...] + jnp.where(half, above, below), 0.0)
    halo = jnp.where(row < terms, halo_flux[...] + jnp.where(half, below, above), 0.0)
    image[...] = value
    to_terms(major, value, value)
    extended = split(marked(jnp.concatenate([value, halo], axis=1), terms))
    coefs = coef_list(coef_own)
    mixed = []
    cuts = list(range(0, nodes, 2 * LANES))
    for part, start in enumerate(cuts):
        span = slice(start, min(start + 2 * LANES, nodes))
        mixed.append(product(*extended, w_high[span, :], w_low[span, :], ((1,), (1,))))
        couple(major, result, coefs, part, len(cuts))
    mixed = jnp.concatenate(mixed, axis=1)
    to_terms(major2, mixed[terms : terms + 1, :] * value - mixed, halo)
    coupled, transferred = from_terms(result, 2)
    coupled = split(jnp.where(row < terms, coupled, 0.0))
    coefs = coef_list(coef_halo)
    flux = []
    cuts = list(range(0, 2 * nodes, 2 * LANES))
    for part, start in enumerate(cuts):
        span = slice(start, start + 2 * LANES)
        flux.append(product(*coupled, w_high[:, span], w_low[:, span], ((1,), (0,))))
        couple(major2, result2, coefs, part, len(cuts))
    flux = jnp.concatenate(flux, axis=1)
    forward, outer = from_terms(result2, 2)
    own = cap[...] * value + transferred + forward - flux[:, 0:nodes]
    own = jnp.where(row < terms, own, 0.0)
    outer = outer - flux[:, nodes:]
    outer = jnp.where(row < terms, outer, 0.0)
    local2[...] = own
    store_sides(near, far, pack(outer, True), pack(outer, False))
    sums = [
        lane_dot(field[...], field[...]),
        lane_dot(field[...], value),
        lane_dot(value, value),
        lane_dot(value, own) + lane_dot(halo, outer),
    ]
    lane = lane_iota((1, LANES))
    packed = jnp.zeros((1, LANES), F32)
    for k, one in enumerate(sums):
        one = one + pltpu.roll(one, LANES // 2, 1)
        one = one + pltpu.roll(one, LANES // 4, 1)
        packed = jnp.where(lane // (LANES // 4) == k, one, packed)
    for peer in range(peers):
        dots[peer] = packed


def final_kernel(
    peers, sends, dots, field, image, local2, got_near, got_far,
    solution_out, residual_out, place, work, out, sems,
):
    terms, nodes = solution_out.shape
    order = order_of(sends)
    blocks = len(order)
    for j in range(blocks):
        place[order[j]] = j
    places = [place[j] for j in range(blocks)]
    total = dots[0]
    for peer in range(1, peers):
        total = total + dots[peer]
    quarter = lane_iota(total.shape) < LANES // 4

    def add(row):
        return jnp.sum(jnp.where(quarter, row, 0.0), axis=1, keepdims=True)

    bb, by, yy, yz = [total] + [pltpu.roll(total, LANES - k * LANES // 4, 1) for k in range(1, 4)]
    norm = add(bb)
    step0 = norm / add(by)
    norm1 = add(bb - step0 * (2.0 * by - step0 * yy))
    ratio = norm1 / norm
    grow = 1.0 + ratio
    curve = add(grow * grow * by - step0 * (grow * (2.0 * yy) - step0 * yz))
    step1 = norm1 / curve
    c1 = step0 + step1 * grow
    c2 = step0 * step1
    copies = []

    def put(which, target):
        for chunk in range(nodes // LANES):
            lanes = slice(chunk * LANES, (chunk + 1) * LANES)
            out[which, :, lanes] = permute_blocks(work.at[which], places, chunk, terms)
        copies.append(pltpu.make_async_copy(out.at[which], target, sems.at[which]))
        copies[-1].start()

    work[0] = c1 * field[...] - c2 * image[...]
    put(0, solution_out)
    below, above = by_side(got_near[...], got_far[...])
    inward = unpack(above, below)
    work[1] = field[...] - c1 * image[...] + c2 * (local2[...] + inward)
    put(1, residual_out)
    for copy in copies:
        copy.wait()


def vmem(count):
    return [pl.BlockSpec(memory_space=pltpu.VMEM)] * count


def hbm(count):
    return [pl.BlockSpec(memory_space=pltpu.HBM)] * count


def smem(count):
    return [pl.BlockSpec(memory_space=pltpu.SMEM)] * count


def in_hbm(value):
    return pltpu.with_memory_space_constraint(value, pltpu.HBM)


def shape(dims, dtype=F32):
    return jax.ShapeDtypeStruct(dims, dtype)


def exchange(near, far):
    count, groups = lax.axis_size("space"), lax.axis_size("grp")
    outer = []
    for group in range(groups):
        start = group * count
        outer += [(start + i, start + (i + 1 if i % 2 else i - 1)) for i in range(1, count - 1)]
        mate = (group ^ 1 if groups % 2 == 0 else group) * count
        ends = (0, count - 1) if groups % 2 == 0 else (count - 1, 0)
        outer += [(start, mate + ends[0]), (start + count - 1, mate + ends[1])]
    inner = [(i, i ^ 1) for i in range(count)]
    got_far = lax.ppermute(far, ("grp", "space"), outer)
    got_near = lax.ppermute(near, "space", inner)
    return got_near, got_far


def shards(right_side, capacity, base_cond, var_field, block_cols, send_list):
    blocks, slots, flat = base_cond.shape
    terms, nodes = right_side.shape
    peers = lax.axis_size("space")
    tall = -(-terms // 8) * 8
    steps = flat // LANES
    params = pltpu.CompilerParams(vmem_limit_bytes=48 * 1024 * 1024)
    wide = shape((tall, nodes))
    piece = shape((packed_rows(tall), LANES))
    coefs = shape((8 * (VARS + 1), LANES))
    weights = shape((nodes, 2 * nodes), BF16)
    spread = pltpu.VMEM((tall * 8, LANES), F32)
    sends = in_hbm(send_list)

    field, near, far = pl.pallas_call(
        send_kernel,
        out_shape=(wide, piece, piece),
        in_specs=hbm(2),
        out_specs=tuple(vmem(3)),
        scratch_shapes=[
            pltpu.SMEM(send_list.shape, jnp.int32),
            pltpu.VMEM((terms, nodes), F32),
            pltpu.SemaphoreType.DMA((2,)),
        ],
        compiler_params=params,
        name="send",
    )(sends, in_hbm(right_side))
    got = exchange(near, far)

    w_high, w_low, part, near_own, flux_halo, coef_own, coef_halo, cap = pl.pallas_call(
        build_kernel,
        out_shape=(weights, weights, wide, wide, wide, coefs, coefs, shape((1, nodes))),
        in_specs=hbm(5) + vmem(1),
        out_specs=tuple(vmem(8)),
        scratch_shapes=[
            pltpu.VMEM((blocks, slots, flat), F32),
            [pltpu.VMEM((2 * blocks, steps, LANES), F32) for _ in range(blocks)],
            pltpu.VMEM((nodes, 2 * nodes), F32),
            spread,
            spread,
            pltpu.VMEM((VARS, nodes), F32),
            pltpu.SMEM(send_list.shape, jnp.int32),
            pltpu.SMEM(block_cols.shape, jnp.int32),
            pltpu.VMEM((1, nodes), F32),
            pltpu.VMEM((VARS, nodes), F32),
            pltpu.SMEM((2 * blocks,), jnp.int32),
            pltpu.SemaphoreType.DMA((slots // 8 + 4,)),
        ],
        compiler_params=params,
        cost_estimate=pl.CostEstimate(flops=10**9, bytes_accessed=4 * 10**6, transcendentals=0),
        name="build",
    )(sends, in_hbm(block_cols), in_hbm(capacity), in_hbm(var_field), in_hbm(base_cond), field)

    local, halo_flux, near, far = pl.pallas_call(
        local_kernel,
        out_shape=(wide, wide, wide, wide),
        in_specs=vmem(9),
        out_specs=tuple(vmem(4)),
        scratch_shapes=[spread] * 2,
        compiler_params=params,
        name="local",
    )(w_high, w_low, field, part, near_own, flux_halo, coef_halo, *got)
    got = exchange(near, far)

    image, local2, near, far, dots = pl.pallas_call(
        functools.partial(second_kernel, peers),
        out_shape=(wide, wide, piece, piece, shape((peers, 1, LANES))),
        in_specs=vmem(10),
        out_specs=tuple(vmem(5)),
        scratch_shapes=[spread] * 4,
        compiler_params=params,
        name="second",
    )(w_high, w_low, field, local, halo_flux, cap, coef_own, coef_halo, *got)
    got = exchange(near, far)
    gathered = lax.all_to_all(dots, "space", 0, 0, tiled=True)

    return pl.pallas_call(
        functools.partial(final_kernel, peers),
        out_shape=(shape((terms, nodes)), shape((terms, nodes))),
        in_specs=smem(1) + vmem(6),
        out_specs=tuple(hbm(2)),
        scratch_shapes=[
            pltpu.SMEM((2 * blocks,), jnp.int32),
            pltpu.VMEM((2, tall, nodes), F32),
            pltpu.VMEM((2, terms, nodes), F32),
            pltpu.SemaphoreType.DMA((2,)),
        ],
        compiler_params=params,
        name="finish",
    )(send_list, gathered, field, image, local2, *got)


def solution(mesh):
    return jax.shard_map(
        shards,
        mesh=mesh,
        in_specs=(
            P(None, ("grp", "space")),
            P(("grp", "space")),
            P(("grp", "space"), None, None),
            P(None, ("grp", "space")),
            P(("grp", "space"), None),
            P(("grp", "space"), None, None),
        ),
        out_specs=(P(None, ("grp", "space")), P(None, ("grp", "space"))),
        check_vma=False,
    )
```

```python
import functools
import math

import jax
import jax.numpy as jnp
from jax import lax
from jax.experimental import pallas as pl
from jax.experimental.pallas import tpu as pltpu
from jax.sharding import PartitionSpec as P

VARS = 8
ORDER = 3
LANES = 128
SPREAD = 0.14
F32 = jnp.float32
BF16 = jnp.bfloat16


@functools.cache
def chaos_links():
    entries = []

    def grow(prefix, budget_left):
        if len(prefix) == VARS:
            entries.append(tuple(prefix))
            return
        for degree in range(budget_left + 1):
            grow(prefix + [degree], budget_left - degree)

    grow([], ORDER)
    entries.sort(key=lambda beta: (sum(beta), tuple(-v for v in beta)))
    lookup = {beta: place for place, beta in enumerate(entries)}
    links = []
    for beta in entries:
        mine = []
        for k in range(VARS):
            if beta[k] > 0:
                lowered = beta[:k] + (beta[k] - 1,) + beta[k + 1 :]
                mine.append((k, lookup[lowered], beta[k]))
            raised = beta[:k] + (beta[k] + 1,) + beta[k + 1 :]
            if raised in lookup:
                mine.append((k, lookup[raised], beta[k] + 1))
        links.append(mine)
    return links


def split(value):
    high = value.astype(BF16)
    return high, (value - high.astype(F32)).astype(BF16)


def product(high, low, w_high, w_low, dims):
    rows = high.shape[0]
    both = jnp.concatenate([high, low], axis=0)
    dot = functools.partial(lax.dot_general, dimension_numbers=(dims, ((), ())), preferred_element_type=F32)
    main = dot(both, w_high)
    return main[:rows] + (main[rows:] + dot(high, w_low))


def couple(source, target, coefs, part=0, parts=1):
    first = coefs[0]
    scaled = {}
    for k in range(VARS):
        for square in range(1, ORDER + 1):
            scaled[k, square] = coefs[k + 1] if square == 1 else coefs[k + 1] * math.sqrt(square)
    links = chaos_links()
    for term in range(part * len(links) // parts, (part + 1) * len(links) // parts):
        mine = links[term]
        total = source[term * 8 : term * 8 + 8, :]
        if first is not None:
            total = total * first
        for k, other, square in mine:
            total = total + scaled[k, square] * source[other * 8 : other * 8 + 8, :]
        target[term * 8 : term * 8 + 8, :] = total


def packed_rows(tall):
    return tall + pack_fold(tall)


def pack_fold(tall):
    return (tall // 2 + 7) // 8 * 8


def pack(value, upper):
    tall = value.shape[0]
    fold = pack_fold(tall)
    middle = value[:, LANES : 2 * LANES]
    head, tail = middle[:fold], pltpu.roll(middle[tall - fold :], LANES // 2, 1)
    low = lower_half(head)
    whole = value[:, 2 * LANES :] if upper else value[:, :LANES]
    return jnp.concatenate([whole, jnp.where(low, tail, head) if upper else jnp.where(low, head, tail)], axis=0)


def unpack(lower, upper):
    tall = lower.shape[0] * 2 // 3 // 8 * 8
    while packed_rows(tall) > lower.shape[0]:
        tall -= 8
    fold = pack_fold(tall)

    def middle(got):
        bent = got[tall:]
        return jnp.concatenate([bent, pltpu.roll(bent, LANES // 2, 1)[2 * fold - tall :]], axis=0)

    first, second = middle(lower), middle(upper)
    return jnp.concatenate([lower[:tall], jnp.where(lower_half(first), first, second), upper[:tall]], axis=1)


def spread_rows(target, chunk, value):
    target[pl.ds(chunk, value.shape[0], stride=8), :] = value


def lane_iota(shape):
    return lax.broadcasted_iota(jnp.int32, shape, len(shape) - 1)


def row_iota(shape):
    return lax.broadcasted_iota(jnp.int32, shape, 0)


def pick_block(ref, place, half, rows):
    tile = ref[0:rows, pl.ds(pl.multiple_of((place // 2) * LANES, LANES), LANES)]
    return jnp.where(place % 2 == half, tile, pltpu.roll(tile, LANES // 2, 1))


def permute_blocks(ref, places, chunk, rows):
    left = pick_block(ref, places[2 * chunk], 0, rows)
    right = pick_block(ref, places[2 * chunk + 1], 1, rows)
    return jnp.where(lane_iota(left.shape) < LANES // 2, left, right)


def marked(value, terms):
    row = row_iota(value.shape)
    return jnp.where(row < terms, value, jnp.where(row == terms, 1.0, 0.0))


def lower_half(value):
    return lane_iota(value.shape) < value.shape[1] // 2


def by_side(near, far):
    place, count = lax.axis_index("space"), lax.axis_size("space")
    far = jnp.where((place == 0) | (place == count - 1), 0.0, far)
    even = place % 2 == 0
    return jnp.where(even, far, near), jnp.where(even, near, far)


def store_sides(near, far, up, down):
    even = lax.axis_index("space") % 2 == 0
    near[...] = jnp.where(even, up, down)
    far[...] = jnp.where(even, down, up)


def transpose8(tiles):
    tiles = [tile if t == 0 else pltpu.roll(tile, t, 0) for t, tile in enumerate(tiles)]
    row = row_iota(tiles[0].shape)
    for bit in (1, 2, 4):
        take = row & bit != 0
        tiles = [jnp.where(take, tiles[(t + bit) % 8], tiles[t]) for t in range(8)]
    return [tiles[0] if k == 0 else pltpu.roll(tiles[8 - k], 8 - k, 0) for k in range(8)]


def to_terms(target, *values):
    tiles = [(value, lane) for value in values for lane in range(0, value.shape[1], LANES)]
    for chunk, (value, lane) in enumerate(tiles):
        spread_rows(target, chunk, value[:, lane : lane + LANES])


def from_terms(source, count):
    rows = source.shape[0] // 8
    return [
        jnp.concatenate([source[pl.ds(3 * i + chunk, rows, stride=8), :] for chunk in range(3)], axis=1)
        for i in range(count)
    ]


def coef_list(ref):
    return [ref[k * 8 : k * 8 + 8, :] for k in range(VARS + 1)]


def set_coefs(ref, first, leading, rest):
    for chunk in range(leading.shape[1] // LANES):
        lanes = slice(chunk * LANES, (chunk + 1) * LANES)
        ref[first + chunk : first + chunk + 1, :] = leading[:, lanes]
        ref[pl.ds(8 + first + chunk, VARS, stride=8), :] = rest[:, lanes]


def lane_dot(a, b):
    lanes_sum = jnp.sum(a * b, axis=0, keepdims=True)
    total = lanes_sum[:, 0:LANES]
    for start in range(LANES, a.shape[1], LANES):
        total = total + lanes_sum[:, start : start + LANES]
    return total


def order_of(sends):
    halves = sends.shape[2]
    return [sends[0, j // halves, j % halves] for j in range(2 * halves)]


def send_kernel(sends_in, field_in, field_p, near, far, sends, field, sems):
    terms, nodes = field_in.shape
    tall = field_p.shape[0]
    copies = [
        pltpu.make_async_copy(sends_in, sends, sems.at[0]),
        pltpu.make_async_copy(field_in, field, sems.at[1]),
    ]
    for copy in copies:
        copy.start()
    for copy in copies:
        copy.wait()
    order = order_of(sends)
    for chunk in range(nodes // LANES):
        lanes = slice(chunk * LANES, (chunk + 1) * LANES)
        field_p[0:terms, lanes] = permute_blocks(field, order, chunk, terms)
        field_p[terms:tall, lanes] = jnp.zeros((tall - terms, LANES), F32)
    value = field_p[...]
    store_sides(near, far, pack(value, False), pack(value, True))


def build_kernel(
    sends_in, cols_in, cap_in, var_in, base, field_p,
    w_high, w_low, flux_own, outer_out, near, far, coef_own, coef_halo, cap_p,
    buf, acc, dense, major, result, weights_p, sends, cols, cap, var, place, sems,
):
    blocks, slots, flat = base.shape
    tall, nodes = field_p.shape
    terms = len(chaos_links())
    width = nodes // blocks
    steps = flat // LANES
    chunks = nodes // LANES
    small = [
        pltpu.make_async_copy(source, target, sems.at[slots // 8 + i])
        for i, (source, target) in enumerate(
            ((sends_in, sends), (cols_in, cols), (cap_in, cap.at[0]), (var_in, var))
        )
    ]
    for copy in small:
        copy.start()
    copies = []
    for i in range(slots // 8):
        some = (slice(None), pl.ds(8 * i, 8))
        copies.append(pltpu.make_async_copy(base.at[some], buf.at[some], sems.at[i]))
        copies[-1].start()
    for copy in small:
        copy.wait()
    order = order_of(sends)
    for j in range(2 * blocks):
        place[j] = j
    for j in range(blocks):
        place[order[j]] = j

    for chunk in range(chunks):
        lanes = slice(chunk * LANES, (chunk + 1) * LANES)
        weights_p[:, lanes] = permute_blocks(var, order, chunk, VARS) * SPREAD
        cap_p[:, lanes] = permute_blocks(cap, order, chunk, 1)
    weights = weights_p[...]
    value = field_p[...]
    for coef in (coef_own, coef_halo):
        coef[...] = jnp.zeros_like(coef)
        set_coefs(coef, 0, jnp.ones((1, nodes), F32), weights)
    to_terms(major, value, value)
    couple(major, result, coef_list(coef_own))

    for one in acc:
        one[...] = jnp.zeros_like(one)
    for slot in range(0, slots, 8):
        copies[slot // 8].wait()
        for j in range(blocks):
            spots = [j if s == 0 else place[cols[order[j], s - 1]] for s in range(slot, slot + 8)]
            for step in range(0, steps, 8):
                tiles = [
                    buf[order[j], slot : slot + 8, t * LANES : (t + 1) * LANES] for t in range(step, step + 8)
                ]
                for spot, tile in zip(spots, transpose8(tiles)):
                    acc[j][spot, step : step + 8, :] += tile
    row = row_iota((8, LANES))
    nigh = lane_iota((8, LANES)) < width
    for j in range(blocks):
        for pair in range(blocks):
            lanes = slice(pair * LANES, (pair + 1) * LANES)
            for step in range(0, steps, 8):
                even = acc[j][2 * pair, step : step + 8, :]
                odd = acc[j][2 * pair + 1, step : step + 8, :]
                first = jnp.where(nigh, even, pltpu.roll(odd, width, 1))
                second = jnp.where(nigh, pltpu.roll(even, width, 1), odd)
                for half in range(2):
                    pick = row // 2 + 4 * half
                    start = j * width + 2 * step + 8 * half
                    dense[start : start + 8, lanes] = jnp.where(
                        row % 2 == 0,
                        jnp.take_along_axis(first, pick, axis=0),
                        jnp.take_along_axis(second, pick, axis=0),
                    )
    for pair in range(blocks):
        lanes = slice(pair * LANES, (pair + 1) * LANES)
        w_high[:, lanes], w_low[:, lanes] = split(dense[:, lanes])

    left = jnp.concatenate([marked(from_terms(result, 1)[0], terms), weights], axis=0)
    flux = product(*split(left), w_high[...], w_low[...], ((1,), (0,)))
    for coef, first, lanes in ((coef_own, chunks, slice(0, nodes)), (coef_halo, chunks, slice(nodes, 2 * nodes))):
        set_coefs(coef, first, flux[terms : terms + 1, lanes], flux[tall : tall + VARS, lanes])
    flux_own[...] = flux[0:tall, 0:nodes]
    outer = flux[:, nodes:]
    outer_out[...] = outer
    store_sides(near, far, pack(outer, True), pack(outer, False))


def local_kernel(
    w_high, w_low, field, flux_own, cap, coef_own, got_near, got_far,
    local, halo_out, near, far, major, result,
):
    terms = len(chaos_links())
    halo = unpack(*by_side(got_near[...], got_far[...]))
    halo_out[...] = halo
    value = field[...]
    row = row_iota(value.shape)
    extended = split(marked(jnp.concatenate([value, halo], axis=1), terms))
    mixed = product(*extended, w_high[...], w_low[...], ((1,), (1,)))
    to_terms(major, mixed[terms : terms + 1, :] * value - mixed, value)
    couple(major, result, coef_list(coef_own))
    forward, transferred = from_terms(result, 2)
    own = jnp.where(row < terms, cap[...] * value + forward + transferred - flux_own[...], 0.0)
    local[...] = own
    store_sides(near, far, pack(own, False), pack(own, True))


def flux_kernel(field, halo, outer, got_near, got_far, inward, outward, coef, major, result):
    tall, nodes = field.shape
    terms = len(chaos_links())
    below, above = by_side(got_near[...], got_far[...])
    inflow = unpack(above, below)
    outer = outer[...]
    coef[...] = jnp.zeros_like(coef)
    for first, flux in ((0, inflow), (nodes // LANES, outer)):
        set_coefs(coef, first, flux[terms : terms + 1, :], flux[tall : tall + VARS, :])
    to_terms(major, field[...], halo[...])
    couple(major, result, coef_list(coef))
    own, other = from_terms(result, 2)
    row = row_iota(own.shape)
    inward[...] = jnp.where(row < terms, own - inflow[0:tall], 0.0)
    outward[...] = jnp.where(row < terms, other - outer[0:tall], 0.0)


def second_kernel(
    peers,
    w_high, w_low, field, local, inward, outward, cap, coef_own, coef_halo, got_near, got_far,
    image, local2, near, far, dots, major, result, major2, result2,
):
    _, nodes = field.shape
    terms = len(chaos_links())
    value = local[...] + inward[...]
    halo = unpack(*by_side(got_near[...], got_far[...])) + outward[...]
    row = row_iota(value.shape)
    image[...] = value
    to_terms(major, value, value)
    extended = split(marked(jnp.concatenate([value, halo], axis=1), terms))
    coefs = coef_list(coef_own)
    mixed = []
    cuts = list(range(0, nodes, 2 * LANES))
    for part, start in enumerate(cuts):
        span = slice(start, min(start + 2 * LANES, nodes))
        mixed.append(product(*extended, w_high[span, :], w_low[span, :], ((1,), (1,))))
        couple(major, result, coefs, part, len(cuts))
    mixed = jnp.concatenate(mixed, axis=1)
    to_terms(major2, mixed[terms : terms + 1, :] * value - mixed, halo)
    coupled, transferred = from_terms(result, 2)
    coupled = split(jnp.where(row < terms, coupled, 0.0))
    coefs = coef_list(coef_halo)
    flux = []
    cuts = list(range(0, 2 * nodes, 2 * LANES))
    for part, start in enumerate(cuts):
        span = slice(start, start + 2 * LANES)
        flux.append(product(*coupled, w_high[:, span], w_low[:, span], ((1,), (0,))))
        couple(major2, result2, coefs, part, len(cuts))
    flux = jnp.concatenate(flux, axis=1)
    forward, outer = from_terms(result2, 2)
    own = cap[...] * value + transferred + forward - flux[:, 0:nodes]
    own = jnp.where(row < terms, own, 0.0)
    outer = outer - flux[:, nodes:]
    outer = jnp.where(row < terms, outer, 0.0)
    local2[...] = own
    store_sides(near, far, pack(outer, True), pack(outer, False))
    sums = [
        lane_dot(field[...], field[...]),
        lane_dot(field[...], value),
        lane_dot(value, value),
        lane_dot(value, own) + lane_dot(halo, outer),
    ]
    lane = lane_iota((1, LANES))
    packed = jnp.zeros((1, LANES), F32)
    for k, one in enumerate(sums):
        one = one + pltpu.roll(one, LANES // 2, 1)
        one = one + pltpu.roll(one, LANES // 4, 1)
        packed = jnp.where(lane // (LANES // 4) == k, one, packed)
    for peer in range(peers):
        dots[peer] = packed


def final_kernel(
    peers, sends, dots, field, image, local2, got_near, got_far,
    solution_out, residual_out, place, work, out, sems,
):
    terms, nodes = solution_out.shape
    order = order_of(sends)
    blocks = len(order)
    for j in range(blocks):
        place[order[j]] = j
    places = [place[j] for j in range(blocks)]
    total = dots[0]
    for peer in range(1, peers):
        total = total + dots[peer]
    quarter = lane_iota(total.shape) < LANES // 4

    def add(row):
        return jnp.sum(jnp.where(quarter, row, 0.0), axis=1, keepdims=True)

    bb, by, yy, yz = [total] + [pltpu.roll(total, LANES - k * LANES // 4, 1) for k in range(1, 4)]
    norm = add(bb)
    step0 = norm / add(by)
    norm1 = add(bb - step0 * (2.0 * by - step0 * yy))
    ratio = norm1 / norm
    grow = 1.0 + ratio
    curve = add(grow * grow * by - step0 * (grow * (2.0 * yy) - step0 * yz))
    step1 = norm1 / curve
    c1 = step0 + step1 * grow
    c2 = step0 * step1
    copies = []

    def put(which, target):
        for chunk in range(nodes // LANES):
            lanes = slice(chunk * LANES, (chunk + 1) * LANES)
            out[which, :, lanes] = permute_blocks(work.at[which], places, chunk, terms)
        copies.append(pltpu.make_async_copy(out.at[which], target, sems.at[which]))
        copies[-1].start()

    work[0] = c1 * field[...] - c2 * image[...]
    put(0, solution_out)
    below, above = by_side(got_near[...], got_far[...])
    inward = unpack(above, below)
    work[1] = field[...] - c1 * image[...] + c2 * (local2[...] + inward)
    put(1, residual_out)
    for copy in copies:
        copy.wait()


def vmem(count):
    return [pl.BlockSpec(memory_space=pltpu.VMEM)] * count


def hbm(count):
    return [pl.BlockSpec(memory_space=pltpu.HBM)] * count


def smem(count):
    return [pl.BlockSpec(memory_space=pltpu.SMEM)] * count


def in_hbm(value):
    return pltpu.with_memory_space_constraint(value, pltpu.HBM)


def shape(dims, dtype=F32):
    return jax.ShapeDtypeStruct(dims, dtype)


def exchange(near, far):
    count, groups = lax.axis_size("space"), lax.axis_size("grp")
    outer = []
    for group in range(groups):
        start = group * count
        outer += [(start + i, start + (i + 1 if i % 2 else i - 1)) for i in range(1, count - 1)]
        mate = (group ^ 1 if groups % 2 == 0 else group) * count
        ends = (0, count - 1) if groups % 2 == 0 else (count - 1, 0)
        outer += [(start, mate + ends[0]), (start + count - 1, mate + ends[1])]
    inner = [(i, i ^ 1) for i in range(count)]
    got_far = lax.ppermute(far, ("grp", "space"), outer)
    got_near = lax.ppermute(near, "space", inner)
    return got_near, got_far


def shards(right_side, capacity, base_cond, var_field, block_cols, send_list):
    blocks, slots, flat = base_cond.shape
    terms, nodes = right_side.shape
    peers = lax.axis_size("space")
    tall = -(-terms // 8) * 8
    steps = flat // LANES
    params = pltpu.CompilerParams(vmem_limit_bytes=48 * 1024 * 1024)
    wide = shape((tall, nodes))
    piece = shape((packed_rows(tall), LANES))
    coefs = shape((8 * (VARS + 1), LANES))
    weights = shape((nodes, 2 * nodes), BF16)
    spread = pltpu.VMEM((tall * 8, LANES), F32)
    sends = in_hbm(send_list)

    field, near, far = pl.pallas_call(
        send_kernel,
        out_shape=(wide, piece, piece),
        in_specs=hbm(2),
        out_specs=tuple(vmem(3)),
        scratch_shapes=[
            pltpu.SMEM(send_list.shape, jnp.int32),
            pltpu.VMEM((terms, nodes), F32),
            pltpu.SemaphoreType.DMA((2,)),
        ],
        compiler_params=params,
        name="send",
    )(sends, in_hbm(right_side))
    got = exchange(near, far)

    tallest = shape((tall + VARS, nodes))
    deep = shape((packed_rows(tall + VARS), LANES))
    w_high, w_low, flux_own, outer, near, far, coef_own, coef_halo, cap = pl.pallas_call(
        build_kernel,
        out_shape=(weights, weights, wide, tallest, deep, deep, coefs, coefs, shape((1, nodes))),
        in_specs=hbm(5) + vmem(1),
        out_specs=tuple(vmem(9)),
        scratch_shapes=[
            pltpu.VMEM((blocks, slots, flat), F32),
            [pltpu.VMEM((2 * blocks, steps, LANES), F32) for _ in range(blocks)],
            pltpu.VMEM((nodes, 2 * nodes), F32),
            spread,
            spread,
            pltpu.VMEM((VARS, nodes), F32),
            pltpu.SMEM(send_list.shape, jnp.int32),
            pltpu.SMEM(block_cols.shape, jnp.int32),
            pltpu.VMEM((1, nodes), F32),
            pltpu.VMEM((VARS, nodes), F32),
            pltpu.SMEM((2 * blocks,), jnp.int32),
            pltpu.SemaphoreType.DMA((slots // 8 + 4,)),
        ],
        compiler_params=params,
        cost_estimate=pl.CostEstimate(flops=10**9, bytes_accessed=4 * 10**6, transcendentals=0),
        name="build",
    )(sends, in_hbm(block_cols), in_hbm(capacity), in_hbm(var_field), in_hbm(base_cond), field)

    got_flux = exchange(near, far)

    local, halo, near, far = pl.pallas_call(
        local_kernel,
        out_shape=(wide, wide, piece, piece),
        in_specs=vmem(8),
        out_specs=tuple(vmem(4)),
        scratch_shapes=[spread] * 2,
        compiler_params=params,
        name="local",
    )(w_high, w_low, field, flux_own, cap, coef_own, *got)
    got = exchange(near, far)
    inward, outward = pl.pallas_call(
        flux_kernel,
        out_shape=(wide, wide),
        in_specs=vmem(5),
        out_specs=tuple(vmem(2)),
        scratch_shapes=[pltpu.VMEM(coefs.shape, F32)] + [spread] * 2,
        compiler_params=params,
        name="flux",
    )(field, halo, outer, *got_flux)

    image, local2, near, far, dots = pl.pallas_call(
        functools.partial(second_kernel, peers),
        out_shape=(wide, wide, piece, piece, shape((peers, 1, LANES))),
        in_specs=vmem(11),
        out_specs=tuple(vmem(5)),
        scratch_shapes=[spread] * 4,
        compiler_params=params,
        name="second",
    )(w_high, w_low, field, local, inward, outward, cap, coef_own, coef_halo, *got)
    got = exchange(near, far)
    gathered = lax.all_to_all(dots, "space", 0, 0, tiled=True)

    return pl.pallas_call(
        functools.partial(final_kernel, peers),
        out_shape=(shape((terms, nodes)), shape((terms, nodes))),
        in_specs=smem(1) + vmem(6),
        out_specs=tuple(hbm(2)),
        scratch_shapes=[
            pltpu.SMEM((2 * blocks,), jnp.int32),
            pltpu.VMEM((2, tall, nodes), F32),
            pltpu.VMEM((2, terms, nodes), F32),
            pltpu.SemaphoreType.DMA((2,)),
        ],
        compiler_params=params,
        name="finish",
    )(send_list, gathered, field, image, local2, *got)


def solution(mesh):
    return jax.shard_map(
        shards,
        mesh=mesh,
        in_specs=(
            P(None, ("grp", "space")),
            P(("grp", "space")),
            P(("grp", "space"), None, None),
            P(None, ("grp", "space")),
            P(("grp", "space"), None),
            P(("grp", "space"), None, None),
        ),
        out_specs=(P(None, ("grp", "space")), P(None, ("grp", "space"))),
        check_vma=False,
    )
```

```python
import functools
import math

import jax
import jax.numpy as jnp
from jax import lax
from jax.experimental import pallas as pl
from jax.experimental.pallas import tpu as pltpu
from jax.sharding import PartitionSpec as P

VARS = 8
ORDER = 3
LANES = 128
SPREAD = 0.14
F32 = jnp.float32
BF16 = jnp.bfloat16


@functools.cache
def chaos_links():
    entries = []

    def grow(prefix, budget_left):
        if len(prefix) == VARS:
            entries.append(tuple(prefix))
            return
        for degree in range(budget_left + 1):
            grow(prefix + [degree], budget_left - degree)

    grow([], ORDER)
    entries.sort(key=lambda beta: (sum(beta), tuple(-v for v in beta)))
    lookup = {beta: place for place, beta in enumerate(entries)}
    links = []
    for beta in entries:
        mine = []
        for k in range(VARS):
            if beta[k] > 0:
                lowered = beta[:k] + (beta[k] - 1,) + beta[k + 1 :]
                mine.append((k, lookup[lowered], beta[k]))
            raised = beta[:k] + (beta[k] + 1,) + beta[k + 1 :]
            if raised in lookup:
                mine.append((k, lookup[raised], beta[k] + 1))
        links.append(mine)
    return links


def split(value):
    high = value.astype(BF16)
    return high, (value - high.astype(F32)).astype(BF16)


def product(high, low, w_high, w_low, dims):
    rows = high.shape[0]
    both = jnp.concatenate([high, low], axis=0)
    dot = functools.partial(lax.dot_general, dimension_numbers=(dims, ((), ())), preferred_element_type=F32)
    main = dot(both, w_high)
    return main[:rows] + (main[rows:] + dot(high, w_low))


def couple(source, target, coefs, part=0, parts=1):
    first = coefs[0]
    scaled = {}
    for k in range(VARS):
        for square in range(1, ORDER + 1):
            scaled[k, square] = coefs[k + 1] if square == 1 else coefs[k + 1] * math.sqrt(square)
    links = chaos_links()
    for term in range(part * len(links) // parts, (part + 1) * len(links) // parts):
        mine = links[term]
        total = source[term * 8 : term * 8 + 8, :]
        if first is not None:
            total = total * first
        for k, other, square in mine:
            total = total + scaled[k, square] * source[other * 8 : other * 8 + 8, :]
        target[term * 8 : term * 8 + 8, :] = total


def packed_rows(tall):
    return tall + pack_fold(tall)


def pack_fold(tall):
    return (tall // 2 + 7) // 8 * 8


def pack(value, upper):
    tall = value.shape[0]
    fold = pack_fold(tall)
    middle = value[:, LANES : 2 * LANES]
    head, tail = middle[:fold], pltpu.roll(middle[tall - fold :], LANES // 2, 1)
    low = lower_half(head)
    whole = value[:, 2 * LANES :] if upper else value[:, :LANES]
    return jnp.concatenate([whole, jnp.where(low, tail, head) if upper else jnp.where(low, head, tail)], axis=0)


def unpack(lower, upper):
    tall = lower.shape[0] * 2 // 3 // 8 * 8
    while packed_rows(tall) > lower.shape[0]:
        tall -= 8
    fold = pack_fold(tall)

    def middle(got):
        bent = got[tall:]
        return jnp.concatenate([bent, pltpu.roll(bent, LANES // 2, 1)[2 * fold - tall :]], axis=0)

    first, second = middle(lower), middle(upper)
    return jnp.concatenate([lower[:tall], jnp.where(lower_half(first), first, second), upper[:tall]], axis=1)


def spread_rows(target, chunk, value):
    target[pl.ds(chunk, value.shape[0], stride=8), :] = value


def lane_iota(shape):
    return lax.broadcasted_iota(jnp.int32, shape, len(shape) - 1)


def row_iota(shape):
    return lax.broadcasted_iota(jnp.int32, shape, 0)


def pick_block(ref, place, half, rows):
    tile = ref[0:rows, pl.ds(pl.multiple_of((place // 2) * LANES, LANES), LANES)]
    return jnp.where(place % 2 == half, tile, pltpu.roll(tile, LANES // 2, 1))


def permute_blocks(ref, places, chunk, rows):
    left = pick_block(ref, places[2 * chunk], 0, rows)
    right = pick_block(ref, places[2 * chunk + 1], 1, rows)
    return jnp.where(lane_iota(left.shape) < LANES // 2, left, right)


def marked(value, terms):
    row = row_iota(value.shape)
    return jnp.where(row < terms, value, jnp.where(row == terms, 1.0, 0.0))


def lower_half(value):
    return lane_iota(value.shape) < value.shape[1] // 2


def by_side(near, far):
    place, count = lax.axis_index("space"), lax.axis_size("space")
    far = jnp.where((place == 0) | (place == count - 1), 0.0, far)
    even = place % 2 == 0
    return jnp.where(even, far, near), jnp.where(even, near, far)


def store_sides(near, far, up, down):
    even = lax.axis_index("space") % 2 == 0
    near[...] = jnp.where(even, up, down)
    far[...] = jnp.where(even, down, up)


def transpose8(tiles):
    tiles = [tile if t == 0 else pltpu.roll(tile, t, 0) for t, tile in enumerate(tiles)]
    row = row_iota(tiles[0].shape)
    for bit in (1, 2, 4):
        take = row & bit != 0
        tiles = [jnp.where(take, tiles[(t + bit) % 8], tiles[t]) for t in range(8)]
    return [tiles[0] if k == 0 else pltpu.roll(tiles[8 - k], 8 - k, 0) for k in range(8)]


def to_terms(target, *values):
    tiles = [(value, lane) for value in values for lane in range(0, value.shape[1], LANES)]
    for chunk, (value, lane) in enumerate(tiles):
        spread_rows(target, chunk, value[:, lane : lane + LANES])


def from_terms(source, count):
    rows = source.shape[0] // 8
    return [
        jnp.concatenate([source[pl.ds(3 * i + chunk, rows, stride=8), :] for chunk in range(3)], axis=1)
        for i in range(count)
    ]


def coef_list(ref):
    return [ref[k * 8 : k * 8 + 8, :] for k in range(VARS + 1)]


def set_coefs(ref, first, leading, rest):
    for chunk in range(leading.shape[1] // LANES):
        lanes = slice(chunk * LANES, (chunk + 1) * LANES)
        ref[first + chunk : first + chunk + 1, :] = leading[:, lanes]
        ref[pl.ds(8 + first + chunk, VARS, stride=8), :] = rest[:, lanes]


def lane_dot(a, b):
    lanes_sum = jnp.sum(a * b, axis=0, keepdims=True)
    total = lanes_sum[:, 0:LANES]
    for start in range(LANES, a.shape[1], LANES):
        total = total + lanes_sum[:, start : start + LANES]
    return total


def order_of(sends):
    halves = sends.shape[2]
    return [sends[0, j // halves, j % halves] for j in range(2 * halves)]


def send_kernel(sends_in, field_in, field_p, near, far, sends, field, sems):
    terms, nodes = field_in.shape
    tall = field_p.shape[0]
    copies = [
        pltpu.make_async_copy(sends_in, sends, sems.at[0]),
        pltpu.make_async_copy(field_in, field, sems.at[1]),
    ]
    for copy in copies:
        copy.start()
    for copy in copies:
        copy.wait()
    order = order_of(sends)
    for chunk in range(nodes // LANES):
        lanes = slice(chunk * LANES, (chunk + 1) * LANES)
        field_p[0:terms, lanes] = permute_blocks(field, order, chunk, terms)
        field_p[terms:tall, lanes] = jnp.zeros((tall - terms, LANES), F32)
    value = field_p[...]
    store_sides(near, far, pack(value, False), pack(value, True))


def build_kernel(
    sends_in, cols_in, cap_in, var_in, base, field_p,
    w_high, w_low, flux_own, outer_out, near, far, coef_own, cap_p,
    buf, acc, dense, major, result, weights_p, sends, cols, cap, var, place, sems,
):
    blocks, slots, flat = base.shape
    tall, nodes = field_p.shape
    terms = len(chaos_links())
    width = nodes // blocks
    steps = flat // LANES
    chunks = nodes // LANES
    small = [
        pltpu.make_async_copy(source, target, sems.at[slots // 8 + i])
        for i, (source, target) in enumerate(
            ((sends_in, sends), (cols_in, cols), (cap_in, cap.at[0]), (var_in, var))
        )
    ]
    for copy in small:
        copy.start()
    copies = []
    for i in range(slots // 8):
        some = (slice(None), pl.ds(8 * i, 8))
        copies.append(pltpu.make_async_copy(base.at[some], buf.at[some], sems.at[i]))
        copies[-1].start()
    for copy in small:
        copy.wait()
    order = order_of(sends)
    for j in range(2 * blocks):
        place[j] = j
    for j in range(blocks):
        place[order[j]] = j

    for chunk in range(chunks):
        lanes = slice(chunk * LANES, (chunk + 1) * LANES)
        weights_p[:, lanes] = permute_blocks(var, order, chunk, VARS) * SPREAD
        cap_p[:, lanes] = permute_blocks(cap, order, chunk, 1)
    weights = weights_p[...]
    value = field_p[...]
    coef_own[...] = jnp.zeros_like(coef_own)
    set_coefs(coef_own, 0, jnp.ones((1, nodes), F32), weights)
    to_terms(major, value, value)
    couple(major, result, coef_list(coef_own))

    for one in acc:
        one[...] = jnp.zeros_like(one)
    for slot in range(0, slots, 8):
        copies[slot // 8].wait()
        for j in range(blocks):
            spots = [j if s == 0 else place[cols[order[j], s - 1]] for s in range(slot, slot + 8)]
            for step in range(0, steps, 8):
                tiles = [
                    buf[order[j], slot : slot + 8, t * LANES : (t + 1) * LANES] for t in range(step, step + 8)
                ]
                for spot, tile in zip(spots, transpose8(tiles)):
                    acc[j][spot, step : step + 8, :] += tile
    row = row_iota((8, LANES))
    nigh = lane_iota((8, LANES)) < width
    for j in range(blocks):
        for pair in range(blocks):
            lanes = slice(pair * LANES, (pair + 1) * LANES)
            for step in range(0, steps, 8):
                even = acc[j][2 * pair, step : step + 8, :]
                odd = acc[j][2 * pair + 1, step : step + 8, :]
                first = jnp.where(nigh, even, pltpu.roll(odd, width, 1))
                second = jnp.where(nigh, pltpu.roll(even, width, 1), odd)
                for half in range(2):
                    pick = row // 2 + 4 * half
                    start = j * width + 2 * step + 8 * half
                    dense[start : start + 8, lanes] = jnp.where(
                        row % 2 == 0,
                        jnp.take_along_axis(first, pick, axis=0),
                        jnp.take_along_axis(second, pick, axis=0),
                    )
    for pair in range(blocks):
        lanes = slice(pair * LANES, (pair + 1) * LANES)
        w_high[:, lanes], w_low[:, lanes] = split(dense[:, lanes])

    left = jnp.concatenate([marked(from_terms(result, 1)[0], terms), weights], axis=0)
    flux = product(*split(left), w_high[...], w_low[...], ((1,), (0,)))
    set_coefs(coef_own, chunks, flux[terms : terms + 1, 0:nodes], flux[tall : tall + VARS, 0:nodes])
    flux_own[...] = flux[0:tall, 0:nodes]
    outer = flux[:, nodes:]
    outer_out[...] = outer
    store_sides(near, far, pack(outer, True), pack(outer, False))


def local_kernel(
    w_high, w_low, field, flux_own, cap, coef_own, got_near, got_far,
    local, halo_out, near, far, major, result,
):
    terms = len(chaos_links())
    halo = unpack(*by_side(got_near[...], got_far[...]))
    halo_out[...] = halo
    value = field[...]
    row = row_iota(value.shape)
    extended = split(marked(jnp.concatenate([value, halo], axis=1), terms))
    mixed = product(*extended, w_high[...], w_low[...], ((1,), (1,)))
    to_terms(major, mixed[terms : terms + 1, :] * value - mixed, value)
    couple(major, result, coef_list(coef_own))
    forward, transferred = from_terms(result, 2)
    own = jnp.where(row < terms, cap[...] * value + forward + transferred - flux_own[...], 0.0)
    local[...] = own
    store_sides(near, far, pack(own, False), pack(own, True))


def flux_kernel(
    w_high, w_low, field, halo, outer, local, cap, coef_own, got_near, got_far,
    image, outward, part, outer2, near, far, coef, coef2, major, result, major2, result2,
):
    tall, nodes = field.shape
    terms = len(chaos_links())
    chunks = nodes // LANES
    below, above = by_side(got_near[...], got_far[...])
    inflow = unpack(above, below)
    outer = outer[...]
    coef[...] = jnp.zeros_like(coef)
    coef2[...] = jnp.zeros_like(coef2)
    transfer = (inflow[terms : terms + 1, :], inflow[tall : tall + VARS, :])
    set_coefs(coef, 0, *transfer)
    set_coefs(coef, chunks, outer[terms : terms + 1, :], outer[tall : tall + VARS, :])
    set_coefs(coef2, chunks, *transfer)
    coef2[...] = coef2[...] + coef_own[...]
    to_terms(major, field[...], halo[...])
    couple(major, result, coef_list(coef))
    own, other = from_terms(result, 2)
    row = row_iota(own.shape)
    outward[...] = jnp.where(row < terms, other - outer[0:tall], 0.0)
    value = local[...] + jnp.where(row < terms, own - inflow[0:tall], 0.0)
    image[...] = value
    to_terms(major2, value, value)
    couple(major2, result2, coef_list(coef2))
    coupled, transferred = from_terms(result2, 2)
    coupled = split(jnp.where(row < terms, coupled, 0.0))
    flux = product(*coupled, w_high[...], w_low[...], ((1,), (0,)))
    part[...] = jnp.where(row < terms, cap[...] * value + transferred - flux[:, 0:nodes], 0.0)
    outer = flux[:, nodes:]
    outer2[...] = outer
    store_sides(near, far, pack(outer, True), pack(outer, False))


def second_kernel(
    peers,
    w_high, w_low, field, image, outward, part, outer2, coef_own, got_near, got_far,
    local2, dots, major, result,
):
    terms = len(chaos_links())
    value = image[...]
    halo = unpack(*by_side(got_near[...], got_far[...])) + outward[...]
    row = row_iota(value.shape)
    extended = split(marked(jnp.concatenate([value, halo], axis=1), terms))
    mixed = product(*extended, w_high[...], w_low[...], ((1,), (1,)))
    to_terms(major, mixed[terms : terms + 1, :] * value - mixed)
    couple(major, result, coef_list(coef_own))
    own = jnp.where(row < terms, part[...] + from_terms(result, 1)[0], 0.0)
    local2[...] = own
    sums = [
        lane_dot(field[...], field[...]),
        lane_dot(field[...], value),
        lane_dot(value, value),
        lane_dot(value, own) - lane_dot(halo, outer2[...]),
    ]
    lane = lane_iota((1, LANES))
    packed = jnp.zeros((1, LANES), F32)
    for k, one in enumerate(sums):
        one = one + pltpu.roll(one, LANES // 2, 1)
        one = one + pltpu.roll(one, LANES // 4, 1)
        packed = jnp.where(lane // (LANES // 4) == k, one, packed)
    for peer in range(peers):
        dots[peer] = packed


def final_kernel(
    peers, sends, dots, field, image, local2, got_near, got_far,
    solution_out, residual_out, place, work, out, sems,
):
    terms, nodes = solution_out.shape
    order = order_of(sends)
    blocks = len(order)
    for j in range(blocks):
        place[order[j]] = j
    places = [place[j] for j in range(blocks)]
    total = dots[0]
    for peer in range(1, peers):
        total = total + dots[peer]
    quarter = lane_iota(total.shape) < LANES // 4

    def add(row):
        return jnp.sum(jnp.where(quarter, row, 0.0), axis=1, keepdims=True)

    bb, by, yy, yz = [total] + [pltpu.roll(total, LANES - k * LANES // 4, 1) for k in range(1, 4)]
    norm = add(bb)
    step0 = norm / add(by)
    norm1 = add(bb - step0 * (2.0 * by - step0 * yy))
    ratio = norm1 / norm
    grow = 1.0 + ratio
    curve = add(grow * grow * by - step0 * (grow * (2.0 * yy) - step0 * yz))
    step1 = norm1 / curve
    c1 = step0 + step1 * grow
    c2 = step0 * step1
    copies = []

    def put(which, target):
        for chunk in range(nodes // LANES):
            lanes = slice(chunk * LANES, (chunk + 1) * LANES)
            out[which, :, lanes] = permute_blocks(work.at[which], places, chunk, terms)
        copies.append(pltpu.make_async_copy(out.at[which], target, sems.at[which]))
        copies[-1].start()

    work[0] = c1 * field[...] - c2 * image[...]
    put(0, solution_out)
    below, above = by_side(got_near[...], got_far[...])
    inward = unpack(above, below)
    work[1] = field[...] - c1 * image[...] + c2 * (local2[...] - inward)
    put(1, residual_out)
    for copy in copies:
        copy.wait()


def vmem(count):
    return [pl.BlockSpec(memory_space=pltpu.VMEM)] * count


def hbm(count):
    return [pl.BlockSpec(memory_space=pltpu.HBM)] * count


def smem(count):
    return [pl.BlockSpec(memory_space=pltpu.SMEM)] * count


def in_hbm(value):
    return pltpu.with_memory_space_constraint(value, pltpu.HBM)


def shape(dims, dtype=F32):
    return jax.ShapeDtypeStruct(dims, dtype)


def exchange(near, far):
    count, groups = lax.axis_size("space"), lax.axis_size("grp")
    outer = []
    for group in range(groups):
        start = group * count
        outer += [(start + i, start + (i + 1 if i % 2 else i - 1)) for i in range(1, count - 1)]
        mate = (group ^ 1 if groups % 2 == 0 else group) * count
        ends = (0, count - 1) if groups % 2 == 0 else (count - 1, 0)
        outer += [(start, mate + ends[0]), (start + count - 1, mate + ends[1])]
    inner = [(i, i ^ 1) for i in range(count)]
    got_far = lax.ppermute(far, ("grp", "space"), outer)
    got_near = lax.ppermute(near, "space", inner)
    return got_near, got_far


def shards(right_side, capacity, base_cond, var_field, block_cols, send_list):
    blocks, slots, flat = base_cond.shape
    terms, nodes = right_side.shape
    peers = lax.axis_size("space")
    tall = -(-terms // 8) * 8
    steps = flat // LANES
    params = pltpu.CompilerParams(vmem_limit_bytes=48 * 1024 * 1024)
    wide = shape((tall, nodes))
    piece = shape((packed_rows(tall), LANES))
    coefs = shape((8 * (VARS + 1), LANES))
    weights = shape((nodes, 2 * nodes), BF16)
    spread = pltpu.VMEM((tall * 8, LANES), F32)
    sends = in_hbm(send_list)

    field, near, far = pl.pallas_call(
        send_kernel,
        out_shape=(wide, piece, piece),
        in_specs=hbm(2),
        out_specs=tuple(vmem(3)),
        scratch_shapes=[
            pltpu.SMEM(send_list.shape, jnp.int32),
            pltpu.VMEM((terms, nodes), F32),
            pltpu.SemaphoreType.DMA((2,)),
        ],
        compiler_params=params,
        name="send",
    )(sends, in_hbm(right_side))
    got = exchange(near, far)

    tallest = shape((tall + VARS, nodes))
    deep = shape((packed_rows(tall + VARS), LANES))
    w_high, w_low, flux_own, outer, near, far, coef_own, cap = pl.pallas_call(
        build_kernel,
        out_shape=(weights, weights, wide, tallest, deep, deep, coefs, shape((1, nodes))),
        in_specs=hbm(5) + vmem(1),
        out_specs=tuple(vmem(8)),
        scratch_shapes=[
            pltpu.VMEM((blocks, slots, flat), F32),
            [pltpu.VMEM((2 * blocks, steps, LANES), F32) for _ in range(blocks)],
            pltpu.VMEM((nodes, 2 * nodes), F32),
            spread,
            spread,
            pltpu.VMEM((VARS, nodes), F32),
            pltpu.SMEM(send_list.shape, jnp.int32),
            pltpu.SMEM(block_cols.shape, jnp.int32),
            pltpu.VMEM((1, nodes), F32),
            pltpu.VMEM((VARS, nodes), F32),
            pltpu.SMEM((2 * blocks,), jnp.int32),
            pltpu.SemaphoreType.DMA((slots // 8 + 4,)),
        ],
        compiler_params=params,
        cost_estimate=pl.CostEstimate(flops=10**9, bytes_accessed=4 * 10**6, transcendentals=0),
        name="build",
    )(sends, in_hbm(block_cols), in_hbm(capacity), in_hbm(var_field), in_hbm(base_cond), field)

    got_flux = exchange(near, far)

    local, halo, near, far = pl.pallas_call(
        local_kernel,
        out_shape=(wide, wide, piece, piece),
        in_specs=vmem(8),
        out_specs=tuple(vmem(4)),
        scratch_shapes=[spread] * 2,
        compiler_params=params,
        name="local",
    )(w_high, w_low, field, flux_own, cap, coef_own, *got)
    got = exchange(near, far)
    image, outward, part, outer2, near, far = pl.pallas_call(
        flux_kernel,
        out_shape=(wide, wide, wide, wide, piece, piece),
        in_specs=vmem(10),
        out_specs=tuple(vmem(6)),
        scratch_shapes=[pltpu.VMEM(coefs.shape, F32)] * 2 + [spread] * 4,
        compiler_params=params,
        name="flux",
    )(w_high, w_low, field, halo, outer, local, cap, coef_own, *got_flux)
    got_flux = exchange(near, far)

    local2, dots = pl.pallas_call(
        functools.partial(second_kernel, peers),
        out_shape=(wide, shape((peers, 1, LANES))),
        in_specs=vmem(10),
        out_specs=tuple(vmem(2)),
        scratch_shapes=[spread] * 2,
        compiler_params=params,
        name="second",
    )(w_high, w_low, field, image, outward, part, outer2, coef_own, *got)
    gathered = lax.all_to_all(dots, "space", 0, 0, tiled=True)

    return pl.pallas_call(
        functools.partial(final_kernel, peers),
        out_shape=(shape((terms, nodes)), shape((terms, nodes))),
        in_specs=smem(1) + vmem(6),
        out_specs=tuple(hbm(2)),
        scratch_shapes=[
            pltpu.SMEM((2 * blocks,), jnp.int32),
            pltpu.VMEM((2, tall, nodes), F32),
            pltpu.VMEM((2, terms, nodes), F32),
            pltpu.SemaphoreType.DMA((2,)),
        ],
        compiler_params=params,
        name="finish",
    )(send_list, gathered, field, image, local2, *got_flux)


def solution(mesh):
    return jax.shard_map(
        shards,
        mesh=mesh,
        in_specs=(
            P(None, ("grp", "space")),
            P(("grp", "space")),
            P(("grp", "space"), None, None),
            P(None, ("grp", "space")),
            P(("grp", "space"), None),
            P(("grp", "space"), None, None),
        ),
        out_specs=(P(None, ("grp", "space")), P(None, ("grp", "space"))),
        check_vma=False,
    )
```

```python
import functools
import math

import jax
import jax.numpy as jnp
from jax import lax
from jax.experimental import pallas as pl
from jax.experimental.pallas import tpu as pltpu
from jax.sharding import PartitionSpec as P

VARS = 8
ORDER = 3
LANES = 128
SPREAD = 0.14
F32 = jnp.float32
BF16 = jnp.bfloat16


@functools.cache
def chaos_links():
    entries = []

    def grow(prefix, budget_left):
        if len(prefix) == VARS:
            entries.append(tuple(prefix))
            return
        for degree in range(budget_left + 1):
            grow(prefix + [degree], budget_left - degree)

    grow([], ORDER)
    entries.sort(key=lambda beta: (sum(beta), tuple(-v for v in beta)))
    lookup = {beta: place for place, beta in enumerate(entries)}
    links = []
    for beta in entries:
        mine = []
        for k in range(VARS):
            if beta[k] > 0:
                lowered = beta[:k] + (beta[k] - 1,) + beta[k + 1 :]
                mine.append((k, lookup[lowered], beta[k]))
            raised = beta[:k] + (beta[k] + 1,) + beta[k + 1 :]
            if raised in lookup:
                mine.append((k, lookup[raised], beta[k] + 1))
        links.append(mine)
    return links


def split(value):
    high = value.astype(BF16)
    return high, (value - high.astype(F32)).astype(BF16)


def product(high, low, w_high, w_low, dims):
    rows = high.shape[0]
    both = jnp.concatenate([high, low], axis=0)
    dot = functools.partial(lax.dot_general, dimension_numbers=(dims, ((), ())), preferred_element_type=F32)
    main = dot(both, w_high)
    return main[:rows] + (main[rows:] + dot(high, w_low))


def couple(source, target, coefs, part=0, parts=1):
    first = coefs[0]
    scaled = {}
    for k in range(VARS):
        for square in range(1, ORDER + 1):
            scaled[k, square] = coefs[k + 1] if square == 1 else coefs[k + 1] * math.sqrt(square)
    links = chaos_links()
    for term in range(part * len(links) // parts, (part + 1) * len(links) // parts):
        mine = links[term]
        total = source[term * 8 : term * 8 + 8, :]
        if first is not None:
            total = total * first
        for k, other, square in mine:
            total = total + scaled[k, square] * source[other * 8 : other * 8 + 8, :]
        target[term * 8 : term * 8 + 8, :] = total


def packed_rows(tall):
    return tall + pack_fold(tall)


def pack_fold(tall):
    return (tall // 2 + 7) // 8 * 8


def pack(value, upper):
    tall = value.shape[0]
    fold = pack_fold(tall)
    middle = value[:, LANES : 2 * LANES]
    head, tail = middle[:fold], pltpu.roll(middle[tall - fold :], LANES // 2, 1)
    low = lower_half(head)
    whole = value[:, 2 * LANES :] if upper else value[:, :LANES]
    return jnp.concatenate([whole, jnp.where(low, tail, head) if upper else jnp.where(low, head, tail)], axis=0)


def unpack(lower, upper):
    tall = lower.shape[0] * 2 // 3 // 8 * 8
    while packed_rows(tall) > lower.shape[0]:
        tall -= 8
    fold = pack_fold(tall)

    def middle(got):
        bent = got[tall:]
        return jnp.concatenate([bent, pltpu.roll(bent, LANES // 2, 1)[2 * fold - tall :]], axis=0)

    first, second = middle(lower), middle(upper)
    return jnp.concatenate([lower[:tall], jnp.where(lower_half(first), first, second), upper[:tall]], axis=1)


def spread_rows(target, chunk, value):
    target[pl.ds(chunk, value.shape[0], stride=8), :] = value


def lane_iota(shape):
    return lax.broadcasted_iota(jnp.int32, shape, len(shape) - 1)


def row_iota(shape):
    return lax.broadcasted_iota(jnp.int32, shape, 0)


def pick_block(ref, place, half, rows):
    tile = ref[0:rows, pl.ds(pl.multiple_of((place // 2) * LANES, LANES), LANES)]
    return jnp.where(place % 2 == half, tile, pltpu.roll(tile, LANES // 2, 1))


def permute_blocks(ref, places, chunk, rows):
    left = pick_block(ref, places[2 * chunk], 0, rows)
    right = pick_block(ref, places[2 * chunk + 1], 1, rows)
    return jnp.where(lane_iota(left.shape) < LANES // 2, left, right)


def marked(value, terms):
    row = row_iota(value.shape)
    return jnp.where(row < terms, value, jnp.where(row == terms, 1.0, 0.0))


def lower_half(value):
    return lane_iota(value.shape) < value.shape[1] // 2


def by_side(near, far):
    place, count = lax.axis_index("space"), lax.axis_size("space")
    far = jnp.where((place == 0) | (place == count - 1), 0.0, far)
    even = place % 2 == 0
    return jnp.where(even, far, near), jnp.where(even, near, far)


def store_sides(near, far, up, down):
    even = lax.axis_index("space") % 2 == 0
    near[...] = jnp.where(even, up, down)
    far[...] = jnp.where(even, down, up)


def transpose8(tiles):
    tiles = [tile if t == 0 else pltpu.roll(tile, t, 0) for t, tile in enumerate(tiles)]
    row = row_iota(tiles[0].shape)
    for bit in (1, 2, 4):
        take = row & bit != 0
        tiles = [jnp.where(take, tiles[(t + bit) % 8], tiles[t]) for t in range(8)]
    return [tiles[0] if k == 0 else pltpu.roll(tiles[8 - k], 8 - k, 0) for k in range(8)]


def to_terms(target, *values):
    tiles = [(value, lane) for value in values for lane in range(0, value.shape[1], LANES)]
    for chunk, (value, lane) in enumerate(tiles):
        spread_rows(target, chunk, value[:, lane : lane + LANES])


def from_terms(source, count):
    rows = source.shape[0] // 8
    return [
        jnp.concatenate([source[pl.ds(3 * i + chunk, rows, stride=8), :] for chunk in range(3)], axis=1)
        for i in range(count)
    ]


def coef_list(ref):
    return [ref[k * 8 : k * 8 + 8, :] for k in range(VARS + 1)]


def set_coefs(ref, first, leading, rest):
    for chunk in range(leading.shape[1] // LANES):
        lanes = slice(chunk * LANES, (chunk + 1) * LANES)
        ref[first + chunk : first + chunk + 1, :] = leading[:, lanes]
        ref[pl.ds(8 + first + chunk, VARS, stride=8), :] = rest[:, lanes]


def lane_dot(a, b):
    lanes_sum = jnp.sum(a * b, axis=0, keepdims=True)
    total = lanes_sum[:, 0:LANES]
    for start in range(LANES, a.shape[1], LANES):
        total = total + lanes_sum[:, start : start + LANES]
    return total


def order_of(sends):
    halves = sends.shape[2]
    return [sends[0, j // halves, j % halves] for j in range(2 * halves)]


def send_kernel(sends_in, field_in, field_p, near, far, sends, field, sems):
    terms, nodes = field_in.shape
    tall = field_p.shape[0]
    copies = [
        pltpu.make_async_copy(sends_in, sends, sems.at[0]),
        pltpu.make_async_copy(field_in, field, sems.at[1]),
    ]
    for copy in copies:
        copy.start()
    for copy in copies:
        copy.wait()
    order = order_of(sends)
    for chunk in range(nodes // LANES):
        lanes = slice(chunk * LANES, (chunk + 1) * LANES)
        field_p[0:terms, lanes] = permute_blocks(field, order, chunk, terms)
        field_p[terms:tall, lanes] = jnp.zeros((tall - terms, LANES), F32)
    value = field_p[...]
    store_sides(near, far, pack(value, False), pack(value, True))


def build_kernel(
    sends_in, cols_in, cap_in, var_in, base, field_p,
    w_high, w_low, flux_own, outer_out, near, far, coef_own, cap_p,
    buf, acc, dense, major, result, weights_p, sends, cols, cap, var, place, sems,
):
    blocks, slots, flat = base.shape
    tall, nodes = field_p.shape
    terms = len(chaos_links())
    width = nodes // blocks
    steps = flat // LANES
    chunks = nodes // LANES
    small = [
        pltpu.make_async_copy(source, target, sems.at[slots // 8 + i])
        for i, (source, target) in enumerate(
            ((sends_in, sends), (cols_in, cols), (cap_in, cap.at[0]), (var_in, var))
        )
    ]
    for copy in small:
        copy.start()
    copies = []
    for i in range(slots // 8):
        some = (slice(None), pl.ds(8 * i, 8))
        copies.append(pltpu.make_async_copy(base.at[some], buf.at[some], sems.at[i]))
        copies[-1].start()
    for copy in small:
        copy.wait()
    order = order_of(sends)
    for j in range(2 * blocks):
        place[j] = j
    for j in range(blocks):
        place[order[j]] = j

    for chunk in range(chunks):
        lanes = slice(chunk * LANES, (chunk + 1) * LANES)
        weights_p[:, lanes] = permute_blocks(var, order, chunk, VARS) * SPREAD
        cap_p[:, lanes] = permute_blocks(cap, order, chunk, 1)
    weights = weights_p[...]
    value = field_p[...]
    coef_own[...] = jnp.zeros_like(coef_own)
    set_coefs(coef_own, 0, jnp.ones((1, nodes), F32), weights)
    to_terms(major, value, value)
    couple(major, result, coef_list(coef_own))

    for one in acc:
        one[...] = jnp.zeros_like(one)
    for slot in range(0, slots, 8):
        copies[slot // 8].wait()
        for j in range(blocks):
            spots = [j if s == 0 else place[cols[order[j], s - 1]] for s in range(slot, slot + 8)]
            for step in range(0, steps, 8):
                tiles = [
                    buf[order[j], slot : slot + 8, t * LANES : (t + 1) * LANES] for t in range(step, step + 8)
                ]
                for spot, tile in zip(spots, transpose8(tiles)):
                    acc[j][spot, step : step + 8, :] += tile
    row = row_iota((8, LANES))
    nigh = lane_iota((8, LANES)) < width
    for j in range(blocks):
        for pair in range(blocks):
            lanes = slice(pair * LANES, (pair + 1) * LANES)
            for step in range(0, steps, 8):
                even = acc[j][2 * pair, step : step + 8, :]
                odd = acc[j][2 * pair + 1, step : step + 8, :]
                first = jnp.where(nigh, even, pltpu.roll(odd, width, 1))
                second = jnp.where(nigh, pltpu.roll(even, width, 1), odd)
                for half in range(2):
                    pick = row // 2 + 4 * half
                    start = j * width + 2 * step + 8 * half
                    dense[start : start + 8, lanes] = jnp.where(
                        row % 2 == 0,
                        jnp.take_along_axis(first, pick, axis=0),
                        jnp.take_along_axis(second, pick, axis=0),
                    )
    for pair in range(blocks):
        lanes = slice(pair * LANES, (pair + 1) * LANES)
        w_high[:, lanes], w_low[:, lanes] = split(dense[:, lanes])

    left = jnp.concatenate([marked(from_terms(result, 1)[0], terms), weights], axis=0)
    flux = product(*split(left), w_high[...], w_low[...], ((1,), (0,)))
    set_coefs(coef_own, chunks, flux[terms : terms + 1, 0:nodes], flux[tall : tall + VARS, 0:nodes])
    flux_own[...] = flux[0:tall, 0:nodes]
    outer = flux[:, nodes:]
    outer_out[...] = outer
    store_sides(near, far, pack(outer, True), pack(outer, False))


def local_kernel(
    w_high, w_low, field, flux_own, cap, coef_own, got_near, got_far,
    local, halo_out, near, far, major, result,
):
    terms = len(chaos_links())
    halo = unpack(*by_side(got_near[...], got_far[...]))
    halo_out[...] = halo
    value = field[...]
    row = row_iota(value.shape)
    extended = split(marked(jnp.concatenate([value, halo], axis=1), terms))
    mixed = product(*extended, w_high[...], w_low[...], ((1,), (1,)))
    to_terms(major, mixed[terms : terms + 1, :] * value - mixed, value)
    couple(major, result, coef_list(coef_own))
    forward, transferred = from_terms(result, 2)
    own = jnp.where(row < terms, cap[...] * value + forward + transferred - flux_own[...], 0.0)
    local[...] = own
    store_sides(near, far, pack(own, False), pack(own, True))


def flux_kernel(
    w_high, w_low, field, halo, outer, local, cap, coef_own, got_near, got_far,
    image, outward, part, outer2, near, far, coef, coef2, major, result, major2, result2,
):
    tall, nodes = field.shape
    terms = len(chaos_links())
    chunks = nodes // LANES
    below, above = by_side(got_near[...], got_far[...])
    inflow = unpack(above, below)
    outer = outer[...]
    coef[...] = jnp.zeros_like(coef)
    coef2[...] = jnp.zeros_like(coef2)
    transfer = (inflow[terms : terms + 1, :], inflow[tall : tall + VARS, :])
    set_coefs(coef, 0, *transfer)
    set_coefs(coef, chunks, outer[terms : terms + 1, :], outer[tall : tall + VARS, :])
    set_coefs(coef2, chunks, *transfer)
    coef2[...] = coef2[...] + coef_own[...]
    to_terms(major, field[...], halo[...])
    couple(major, result, coef_list(coef))
    own, other = from_terms(result, 2)
    row = row_iota(own.shape)
    outward[...] = jnp.where(row < terms, other - outer[0:tall], 0.0)
    value = local[...] + jnp.where(row < terms, own - inflow[0:tall], 0.0)
    image[...] = value
    to_terms(major2, value, value)
    couple(major2, result2, coef_list(coef2))
    coupled, transferred = from_terms(result2, 2)
    coupled = split(jnp.where(row < terms, coupled, 0.0))
    flux = product(*coupled, w_high[...], w_low[...], ((1,), (0,)))
    part[...] = jnp.where(row < terms, cap[...] * value + transferred - flux[:, 0:nodes], 0.0)
    outer = flux[:, nodes:]
    outer2[...] = outer
    store_sides(near, far, pack(outer, True), pack(outer, False))


def second_kernel(
    peers,
    w_high, w_low, field, image, outward, part, outer2, coef_own, got_near, got_far,
    local2, dots, major, result,
):
    terms = len(chaos_links())
    value = image[...]
    halo = unpack(*by_side(got_near[...], got_far[...])) + outward[...]
    row = row_iota(value.shape)
    extended = split(marked(jnp.concatenate([value, halo], axis=1), terms))
    mixed = product(*extended, w_high[...], w_low[...], ((1,), (1,)))
    to_terms(major, mixed[terms : terms + 1, :] * value - mixed)
    couple(major, result, coef_list(coef_own))
    own = jnp.where(row < terms, part[...] + from_terms(result, 1)[0], 0.0)
    local2[...] = own
    sums = [
        lane_dot(field[...], field[...]),
        lane_dot(field[...], value),
        lane_dot(value, value),
        lane_dot(value, own) - lane_dot(halo, outer2[...]),
    ]
    lane = lane_iota((1, LANES))
    packed = jnp.zeros((1, LANES), F32)
    for k, one in enumerate(sums):
        one = one + pltpu.roll(one, LANES // 2, 1)
        one = one + pltpu.roll(one, LANES // 4, 1)
        packed = jnp.where(lane // (LANES // 4) == k, one, packed)
    for peer in range(peers):
        dots[peer] = packed


def step_kernel(peers, dots, steps):
    total = dots[0]
    for peer in range(1, peers):
        total = total + dots[peer]
    quarter = lane_iota(total.shape) < LANES // 4

    def add(row):
        return jnp.sum(jnp.where(quarter, row, 0.0), axis=1, keepdims=True)

    bb, by, yy, yz = [total] + [pltpu.roll(total, LANES - k * LANES // 4, 1) for k in range(1, 4)]
    norm = add(bb)
    step0 = norm / add(by)
    norm1 = add(bb - step0 * (2.0 * by - step0 * yy))
    ratio = norm1 / norm
    grow = 1.0 + ratio
    curve = add(grow * grow * by - step0 * (grow * (2.0 * yy) - step0 * yz))
    step1 = norm1 / curve
    c1 = step0 + step1 * grow
    c2 = step0 * step1
    steps[...] = jnp.where(row_iota(steps.shape) == 0, c1, c2)


def final_kernel(
    sends, steps, field, image, local2, got_near, got_far,
    solution_out, residual_out, place, work, out, sems,
):
    terms, nodes = solution_out.shape
    order = order_of(sends)
    blocks = len(order)
    for j in range(blocks):
        place[order[j]] = j
    places = [place[j] for j in range(blocks)]
    c1, c2 = steps[0:1, 0:1], steps[1:2, 0:1]
    copies = []

    def put(which, target):
        for chunk in range(nodes // LANES):
            lanes = slice(chunk * LANES, (chunk + 1) * LANES)
            out[which, :, lanes] = permute_blocks(work.at[which], places, chunk, terms)
        copies.append(pltpu.make_async_copy(out.at[which], target, sems.at[which]))
        copies[-1].start()

    work[0] = c1 * field[...] - c2 * image[...]
    put(0, solution_out)
    below, above = by_side(got_near[...], got_far[...])
    inward = unpack(above, below)
    work[1] = field[...] - c1 * image[...] + c2 * (local2[...] - inward)
    put(1, residual_out)
    for copy in copies:
        copy.wait()


def vmem(count):
    return [pl.BlockSpec(memory_space=pltpu.VMEM)] * count


def hbm(count):
    return [pl.BlockSpec(memory_space=pltpu.HBM)] * count


def smem(count):
    return [pl.BlockSpec(memory_space=pltpu.SMEM)] * count


def in_hbm(value):
    return pltpu.with_memory_space_constraint(value, pltpu.HBM)


def shape(dims, dtype=F32):
    return jax.ShapeDtypeStruct(dims, dtype)


def exchange(near, far):
    count, groups = lax.axis_size("space"), lax.axis_size("grp")
    outer = []
    for group in range(groups):
        start = group * count
        outer += [(start + i, start + (i + 1 if i % 2 else i - 1)) for i in range(1, count - 1)]
        mate = (group ^ 1 if groups % 2 == 0 else group) * count
        ends = (0, count - 1) if groups % 2 == 0 else (count - 1, 0)
        outer += [(start, mate + ends[0]), (start + count - 1, mate + ends[1])]
    inner = [(i, i ^ 1) for i in range(count)]
    got_far = lax.ppermute(far, ("grp", "space"), outer)
    got_near = lax.ppermute(near, "space", inner)
    return got_near, got_far


def shards(right_side, capacity, base_cond, var_field, block_cols, send_list):
    blocks, slots, flat = base_cond.shape
    terms, nodes = right_side.shape
    peers = lax.axis_size("space")
    tall = -(-terms // 8) * 8
    steps = flat // LANES
    params = pltpu.CompilerParams(vmem_limit_bytes=48 * 1024 * 1024)
    wide = shape((tall, nodes))
    piece = shape((packed_rows(tall), LANES))
    coefs = shape((8 * (VARS + 1), LANES))
    weights = shape((nodes, 2 * nodes), BF16)
    spread = pltpu.VMEM((tall * 8, LANES), F32)
    sends = in_hbm(send_list)

    field, near, far = pl.pallas_call(
        send_kernel,
        out_shape=(wide, piece, piece),
        in_specs=hbm(2),
        out_specs=tuple(vmem(3)),
        scratch_shapes=[
            pltpu.SMEM(send_list.shape, jnp.int32),
            pltpu.VMEM((terms, nodes), F32),
            pltpu.SemaphoreType.DMA((2,)),
        ],
        compiler_params=params,
        name="send",
    )(sends, in_hbm(right_side))
    got = exchange(near, far)

    tallest = shape((tall + VARS, nodes))
    deep = shape((packed_rows(tall + VARS), LANES))
    w_high, w_low, flux_own, outer, near, far, coef_own, cap = pl.pallas_call(
        build_kernel,
        out_shape=(weights, weights, wide, tallest, deep, deep, coefs, shape((1, nodes))),
        in_specs=hbm(5) + vmem(1),
        out_specs=tuple(vmem(8)),
        scratch_shapes=[
            pltpu.VMEM((blocks, slots, flat), F32),
            [pltpu.VMEM((2 * blocks, steps, LANES), F32) for _ in range(blocks)],
            pltpu.VMEM((nodes, 2 * nodes), F32),
            spread,
            spread,
            pltpu.VMEM((VARS, nodes), F32),
            pltpu.SMEM(send_list.shape, jnp.int32),
            pltpu.SMEM(block_cols.shape, jnp.int32),
            pltpu.VMEM((1, nodes), F32),
            pltpu.VMEM((VARS, nodes), F32),
            pltpu.SMEM((2 * blocks,), jnp.int32),
            pltpu.SemaphoreType.DMA((slots // 8 + 4,)),
        ],
        compiler_params=params,
        cost_estimate=pl.CostEstimate(flops=10**9, bytes_accessed=4 * 10**6, transcendentals=0),
        name="build",
    )(sends, in_hbm(block_cols), in_hbm(capacity), in_hbm(var_field), in_hbm(base_cond), field)

    got_flux = exchange(near, far)

    local, halo, near, far = pl.pallas_call(
        local_kernel,
        out_shape=(wide, wide, piece, piece),
        in_specs=vmem(8),
        out_specs=tuple(vmem(4)),
        scratch_shapes=[spread] * 2,
        compiler_params=params,
        name="local",
    )(w_high, w_low, field, flux_own, cap, coef_own, *got)
    got = exchange(near, far)
    image, outward, part, outer2, near, far = pl.pallas_call(
        flux_kernel,
        out_shape=(wide, wide, wide, wide, piece, piece),
        in_specs=vmem(10),
        out_specs=tuple(vmem(6)),
        scratch_shapes=[pltpu.VMEM(coefs.shape, F32)] * 2 + [spread] * 4,
        compiler_params=params,
        name="flux",
    )(w_high, w_low, field, halo, outer, local, cap, coef_own, *got_flux)
    got_flux = exchange(near, far)

    local2, dots = pl.pallas_call(
        functools.partial(second_kernel, peers),
        out_shape=(wide, shape((peers, 1, LANES))),
        in_specs=vmem(10),
        out_specs=tuple(vmem(2)),
        scratch_shapes=[spread] * 2,
        compiler_params=params,
        name="second",
    )(w_high, w_low, field, image, outward, part, outer2, coef_own, *got)
    gathered = lax.all_to_all(dots, "space", 0, 0, tiled=True)

    step_sizes = pl.pallas_call(
        functools.partial(step_kernel, peers),
        out_shape=shape((8, LANES)),
        in_specs=vmem(1),
        out_specs=vmem(1)[0],
        compiler_params=params,
        name="step",
    )(gathered)

    return pl.pallas_call(
        final_kernel,
        out_shape=(shape((terms, nodes)), shape((terms, nodes))),
        in_specs=smem(1) + vmem(6),
        out_specs=tuple(hbm(2)),
        scratch_shapes=[
            pltpu.SMEM((2 * blocks,), jnp.int32),
            pltpu.VMEM((2, tall, nodes), F32),
            pltpu.VMEM((2, terms, nodes), F32),
            pltpu.SemaphoreType.DMA((2,)),
        ],
        compiler_params=params,
        name="finish",
    )(send_list, step_sizes, field, image, local2, *got_flux)


def solution(mesh):
    return jax.shard_map(
        shards,
        mesh=mesh,
        in_specs=(
            P(None, ("grp", "space")),
            P(("grp", "space")),
            P(("grp", "space"), None, None),
            P(None, ("grp", "space")),
            P(("grp", "space"), None),
            P(("grp", "space"), None, None),
        ),
        out_specs=(P(None, ("grp", "space")), P(None, ("grp", "space"))),
        check_vma=False,
    )
```
